256 devices in a mesh: sub: 32 (over x, z), site: 8 (over y, core).
Axes of the slice: x: 4, y: 4, z: 8, core: 2. Of those that a mesh axis runs over, the one named last changes fastest.
Arguments:
- sgt: bfloat16 [2048, 2, 2, 6, 128, 128], P('sub', None, None, None, 'site'), may hold values from -6 to 6
- mechanism: float32 [2048, 6], P('sub'), may hold values from -5 to 5
- slip: bfloat16 [2048, 64, 2, 128], P('sub'), may hold values from -0.109375 to 0.109375
- point_list: int32 [2048], replicated, may hold values from 0 to 2047, as said below
- subfault_counts: int32 [32], replicated, may hold values from 1 to 64, 1024 in all
Outputs:
- seismograms: bfloat16 [64, 2, 128, 2048], P('sub', None, 'site')
- psa: float32 [64, 2, 128, 40], P('sub', None, 'site')
The draws below stay inside these ranges and needn't reach their ends.
Inputs may be any that keep to these rules, and one draw needn't show every extreme that they name: `point_list`: every SGT point is named by exactly one subfault slot. Of the 64 slots of each worker w (slots w * 64 to w * 64 + 63), exactly 2 name points of each reader block r (points r * 64 to r * 64 + 63). `subfault_counts`: the counts sum to 1024, and the largest is 64. Slots of a worker past its count are not part of the rupture.
All inputs are finite; a program needn't handle non-finite values.
Results may differ from the reference program's by a relative error of at most 0.0049.
Values may be sent and summed in bfloat16 or wider, within the bound.
A program may use at most 128 MiB of HBM per device.

```python
import math
import jax
import jax.numpy as jnp
import numpy as np
from jax import lax

NT = 2048
FREQS = 128
VARS = 64
PERIODS = 40
CAP = 2
WORKERS = 32
SLOTS = 64
PT_DEV = 64
SUBFAULTS = 2048
POINTS = 2048
SITES = 128


def draw_point_list(key, part):
    reader_key, row_key = jax.random.split(key)
    base_readers = jnp.repeat(jnp.arange(WORKERS, dtype=jnp.int32), CAP)
    tiled_ids = jnp.tile(base_readers[None, :], (WORKERS, 1))
    readers = jax.random.permutation(reader_key, tiled_ids, axis=1, independent=True)
    onehot = (readers[:, :, None] == jnp.arange(WORKERS, dtype=jnp.int32)[None, None, :]).astype(jnp.int32)
    occurrence = jnp.sum(onehot * jnp.cumsum(onehot, axis=1), axis=2) - 1
    base_rows = jnp.tile(jnp.arange(PT_DEV, dtype=jnp.int32)[None, :], (WORKERS, 1))
    row_perm = jax.random.permutation(row_key, base_rows, axis=1, independent=True)
    request = jnp.arange(WORKERS, dtype=jnp.int32)[:, None] * CAP + occurrence
    row_ids = row_perm[readers, request]
    return (readers * PT_DEV + row_ids).reshape(-1).astype(jnp.int32)


def raised(result, stream_key, source, target, blocks, factor):
    def block_of(dim):
        return (jnp.arange(result.shape[dim]) // (result.shape[dim] // blocks)).reshape((-1,) + (1,) * (result.ndim - 1 - dim))

    near = jax.random.permutation(stream_key, blocks)[block_of(target)]
    second = (block_of(target) + blocks // 2) % blocks
    return jnp.where((block_of(source) == near) | (block_of(source) == second), factor * result, result)


def levels(rng, dims, shards, least, largest):
    level, own = 1.0, jax.random.fold_in(rng, 6)
    for position, blocks in shards:
        heights = jnp.exp(jax.random.uniform(jax.random.fold_in(own, position), (blocks,), jnp.float32, least / len(shards), largest / len(shards)))
        level = level * jnp.repeat(heights, dims[position] // blocks).reshape([-1 if axis == position else 1 for axis in range(len(dims))])
    return level


def split_up(amount, total, most, slope):
    loads = [(1 << 20) // math.isqrt(rank ** slope) + 1 for rank in range(2, amount + 1)]
    rest, counts = total - most - (amount - 1), [1] * (amount - 1)
    while rest > 0:
        candidates = [i for i in range(amount - 1) if counts[i] < most]
        mass, budget = sum([loads[i] for i in candidates]), rest
        for i in candidates:
            extra = min(most - counts[i], max(1, budget * loads[i] // mass), rest)
            counts[i] = counts[i] + extra
            rest = rest - extra
    return np.array([most] + counts)


def uneven_parts(stream_key, number_of, total, reach, slope):
    if number_of == 2:
        one = jax.random.randint(stream_key, (), max(1, total - reach), min(reach, total - 1) + 1)
        return jnp.stack([one, total - one])
    lengths = jnp.asarray(split_up(number_of, total, reach, slope), jnp.int32)
    pairs = (number_of - 1) // 2
    source_of, sink = lengths[1:1 + 2 * pairs:2], lengths[2:2 + 2 * pairs:2]
    margin = jnp.minimum(source_of - 1, reach - sink)
    shifted = jax.random.randint(jax.random.fold_in(stream_key, 1), (pairs,), 0, 1 << 20) % (margin + 1)
    lengths = lengths.at[1:1 + 2 * pairs:2].set(source_of - shifted).at[2:2 + 2 * pairs:2].set(sink + shifted)
    return lengths[jax.random.permutation(jax.random.fold_in(stream_key, 2), number_of)]


def gaussian(stream_key, extent, spread, bound, cuts=(), kind=jnp.bfloat16):
    result = spread * jax.random.normal(stream_key, extent, jnp.float32)
    if cuts:
        result = result * levels(stream_key, extent, cuts, -0.22, 0.18)
    return jnp.clip(result, -bound, bound).astype(kind)


def gaussian_with(stream_key, extent, scale, reach, cuts, heavy, kind=jnp.bfloat16):
    values = scale * jax.random.normal(stream_key, extent, jnp.float32)
    if cuts:
        values = values * levels(stream_key, extent, cuts, -0.22, 0.18)
    return jnp.clip(raised(values, jax.random.fold_in(stream_key, 3), *heavy), -reach, reach).astype(kind)


def setup_inputs(seed: int = 0) -> dict:
    key_list = jax.random.split(jax.random.key(seed), 6)
    return {
        "sgt": gaussian(key_list[0], (POINTS, 2, 2, 6, SITES, FREQS), 1.0, 6.0, ((0, 32), (4, 8))),
        "mechanism": gaussian(key_list[1], (SUBFAULTS, 6), 1.0, 5.0, ((0, 32),), jnp.float32),
        "slip": gaussian_with(key_list[2], (SUBFAULTS, VARS, 2, FREQS), (6 * SUBFAULTS) ** -0.5, 0.109375, ((0, 32),), (0, 1, 32, 2.75)),
        "point_list": draw_point_list(jax.random.fold_in(key_list[5], 71), 0),
        "subfault_counts": uneven_parts(key_list[4], WORKERS, SUBFAULTS // 2, SLOTS, 2).astype(jnp.int32),
    }


damping = 0.05
sample_step = 0.1

def synthesis_basis(freq_count, sample_count):
    freq_ids = jnp.arange(freq_count, dtype=jnp.int32)
    time_ids = jnp.arange(sample_count, dtype=jnp.int32)
    angles = (freq_ids[:, None] * time_ids[None, :] % sample_count).astype(jnp.float32) * (2.0 * math.pi / sample_count)
    norm_scale = 1.0 / math.sqrt(freq_count)
    return jnp.stack([norm_scale * jnp.cos(angles), -norm_scale * jnp.sin(angles)])

def oscillator_gains(period_count, freq_count, sample_count):
    period_ids = jnp.arange(period_count, dtype=jnp.float32)
    periods = 2.0 * jnp.exp(period_ids * (math.log(5.0) / max(period_count - 1, 1)))
    natural = 2.0 * math.pi / periods
    omega_bins = jnp.arange(freq_count, dtype=jnp.float32) * (2.0 * math.pi / (sample_count * sample_step))
    squared_natural = (natural * natural)[:, None]
    real_part = squared_natural - (omega_bins * omega_bins)[None, :]
    imag_part = 2.0 * damping * natural[:, None] * omega_bins[None, :]
    magnitude = real_part * real_part + imag_part * imag_part
    return (-squared_natural * real_part / magnitude, squared_natural * imag_part / magnitude)

def reference(sgt, mechanism, slip, point_list, subfault_counts):
    slot_ids = jnp.arange(SUBFAULTS, dtype=jnp.int32)
    owner_ids = slot_ids // SLOTS
    valid_mask = slot_ids % SLOTS < jnp.take(subfault_counts, owner_ids)
    slip_live = slip * valid_mask.astype(slip.dtype)[:, None, None, None]

    def add_block(running, block_index):
        block_start = block_index * SLOTS
        point_rows = lax.dynamic_slice_in_dim(point_list, block_start, SLOTS)
        green_rows = jnp.take(sgt, point_rows, axis=0).astype(jnp.float32)
        moments = lax.dynamic_slice_in_dim(mechanism, block_start, SLOTS)
        combined = moments[:, 0, None, None, None, None] * green_rows[:, :, :, 0]
        for strain in range(1, 6):
            combined = combined + moments[:, strain, None, None, None, None] * green_rows[:, :, :, strain]
        projected = lax.optimization_barrier(combined.astype(jnp.bfloat16)).astype(jnp.float32)
        slip_block = lax.dynamic_slice_in_dim(slip_live, block_start, SLOTS).astype(jnp.float32)
        with_real = jnp.einsum('jrcsf,jvf->rvcsf', projected, slip_block[:, :, 0], precision=lax.Precision.HIGHEST)
        with_imag = jnp.einsum('jrcsf,jvf->rvcsf', projected, slip_block[:, :, 1], precision=lax.Precision.HIGHEST)
        update = jnp.stack([with_real[0] - with_imag[1], with_imag[0] + with_real[1]], axis=2)
        return (running + update, None)
    start_value = jnp.zeros((VARS, 2, 2, SITES, FREQS), jnp.float32)
    spectrum = lax.scan(add_block, start_value, jnp.arange(WORKERS, dtype=jnp.int32))[0]
    basis = synthesis_basis(FREQS, NT)
    motion = jnp.einsum('vcrsf,rft->vcst', spectrum, basis, precision=lax.Precision.HIGHEST)
    seismograms = motion.astype(jnp.bfloat16)
    gain_real, gain_imag = oscillator_gains(PERIODS, FREQS, NT)
    basis_low = lax.optimization_barrier(basis.astype(jnp.bfloat16)).astype(jnp.float32)
    spec_real = spectrum[:, :, 0]
    spec_imag = spectrum[:, :, 1]

    def one_period(gains):
        resp_real = gains[0] * spec_real - gains[1] * spec_imag
        resp_imag = gains[0] * spec_imag + gains[1] * spec_real
        response = jnp.stack([resp_real, resp_imag], axis=2).astype(jnp.bfloat16)
        response = lax.optimization_barrier(response).astype(jnp.float32)
        response_wave = jnp.einsum('vcrsf,rft->vcst', response, basis_low, precision=lax.Precision.HIGHEST)
        return lax.optimization_barrier(jnp.max(jnp.abs(response_wave), axis=3))
    peak_values = lax.map(one_period, jnp.stack([gain_real, gain_imag], axis=1))
    return (seismograms, jnp.transpose(peak_values, (1, 2, 3, 0)))
```

```python
import functools
import math

import jax
import jax.numpy as jnp
import numpy as np
from jax import lax
from jax.experimental import pallas as pl
from jax.experimental.pallas import tpu as pltpu
from jax.sharding import PartitionSpec as P

NT = 2048
PERIODS = 40
CHUNKS = 2
MESH = pl.DeviceIdType.MESH

damping = 0.05
sample_step = 0.1


def bins_in_order(freq_count):
    kappa = np.arange(freq_count)
    quarter = freq_count // 4
    return 4 * (kappa % quarter) + kappa // quarter


def synthesis_basis(freq_count, sample_count):
    freq_ids = bins_in_order(freq_count)
    angles = (freq_ids[:, None] * np.arange(sample_count)[None, :] % sample_count) * (2.0 * math.pi / sample_count)
    scale = 1.0 / math.sqrt(freq_count)
    both = np.concatenate([scale * np.cos(angles), -scale * np.sin(angles)], axis=0).astype(np.float32)
    high = both.astype(jnp.bfloat16)
    low = (both - high.astype(np.float32)).astype(jnp.bfloat16)
    return high, low


def oscillator_gains(period_count, freq_count, sample_count):
    periods = 2.0 * np.exp(np.arange(period_count) * (math.log(5.0) / max(period_count - 1, 1)))
    natural = 2.0 * math.pi / periods
    omega = bins_in_order(freq_count) * (2.0 * math.pi / (sample_count * sample_step))
    squared = (natural * natural)[:, None]
    real_part = squared - (omega * omega)[None, :]
    imag_part = 2.0 * damping * natural[:, None] * omega[None, :]
    magnitude = real_part * real_part + imag_part * imag_part
    return np.stack([-squared * real_part / magnitude, squared * imag_part / magnitude]).astype(np.float32)


def spectrum_kernel(
    dims, points_ref, counts_ref, mech_ref, slip_hbm, sgt_hbm, spec_ref,
    table, table_smem, sgt, slip, mech_out, mech_in, wide, slip_out, slip_in, flip, proj_out, proj_in,
    pieces, piece_flip, part, part_out, part_in,
    table_sem, sgt_sem, slip_sem, mech_ssem, mech_rsem, slip_ssem, slip_rsem, proj_ssem, proj_rsem,
    ring_ssem, ring_rsem, pair_ssem, pair_rsem, part_ssem, part_rsem,
):
    nx, nz, ny = dims
    workers = nx * nz
    slots, vq, freqs = slip.shape
    rows_pc = 2 * 2 * sgt.shape[4]
    per_reader = sgt.shape[0]
    share = freqs // nx
    group = workers // CHUNKS
    packs = points_ref.shape[1] // slots
    table_rows = points_ref.shape[0]
    lanes = points_ref.shape[1]

    me = lax.axis_index("sub")
    site = lax.axis_index("site")
    my_x = me // nz
    my_y = site // 2
    core = site % 2

    get_slip = pltpu.make_async_copy(slip_hbm, slip, slip_sem)
    get_slip.start()
    get_sgt = pltpu.make_async_copy(sgt_hbm, sgt, sgt_sem)
    get_sgt.start()

    def peer_of(step):
        return lax.rem(me + step, workers)

    def site_of(step):
        return lax.rem(my_y + step, ny) * 2 + core

    other = my_y * 2 + (1 - core)

    barrier = pltpu.get_barrier_semaphore()

    @pl.loop(1, workers)
    def _(step):
        pl.semaphore_signal(barrier, inc=1, device_id={"sub": peer_of(step)}, device_id_type=MESH)

    for step in range(1, ny):
        pl.semaphore_signal(barrier, inc=1, device_id={"site": site_of(step)}, device_id_type=MESH)
    pl.semaphore_signal(barrier, inc=1, device_id={"site": other}, device_id_type=MESH)

    points = points_ref[...]
    lane = lax.broadcasted_iota(jnp.int32, (table_rows, lanes), 1)
    out_lane = lax.broadcasted_iota(jnp.int32, (table_rows, 128), 1)
    mine = points // per_reader == me
    local = points % per_reader
    named = jnp.zeros((table_rows, 128), jnp.int32)
    for pack in range(packs):
        here = mine & (lane // slots == pack)
        first = jnp.min(jnp.where(here, lane, lanes), axis=1, keepdims=True)
        last = jnp.max(jnp.where(here, lane, -1), axis=1, keepdims=True)
        for k, found in enumerate((first, last)):
            row = jnp.sum(jnp.where(here & (lane == found), local, 0), axis=1, keepdims=True)
            named = jnp.where(out_lane == pack * 2 + k, row, named)
    table[pl.ds(0, table_rows), :] = named

    my_points = points_ref[pl.ds(me // packs, 1), :]
    lane = lax.broadcasted_iota(jnp.int32, (workers, lanes), 1)
    out_lane = lax.broadcasted_iota(jnp.int32, (workers, 128), 1)
    reader = lax.broadcasted_iota(jnp.int32, (workers, lanes), 0)
    base = lax.rem(me, packs) * slots
    here = (my_points // per_reader == reader) & (lane >= base) & (lane < base + slots)
    first = jnp.min(jnp.where(here, lane, lanes), axis=1, keepdims=True)
    last = jnp.max(jnp.where(here, lane, -1), axis=1, keepdims=True)
    table[pl.ds(table_rows, workers), :] = jnp.clip(jnp.where(out_lane == 0, first, last) - base, 0, slots - 1)
    to_smem = pltpu.make_async_copy(table, table_smem, table_sem)
    to_smem.start()

    live = lane - base < counts_ref[me]
    moments = jnp.concatenate([mech_ref[...]] * packs, axis=1)
    sent = jnp.zeros((workers, 128), jnp.float32)
    for k, found in enumerate((first, last)):
        chosen = here & live & (lane == found)
        for m in range(6):
            value = jnp.sum(jnp.where(chosen, moments[m : m + 1, :], 0.0), axis=1, keepdims=True)
            sent = jnp.where(out_lane == k * 6 + m, value, sent)
    mech_out[...] = sent.reshape(workers, 1, 128)

    to_smem.wait()
    get_slip.wait()
    my_k = site // nx
    x_of_piece = lax.rem(site, nx)

    @pl.loop(0, nz)
    def _(zr):
        slot = table_smem[table_rows + x_of_piece * nz + zr, my_k]
        turned = slip[slot].astype(jnp.float32).T.astype(jnp.bfloat16)
        for x in range(nx):
            slip_out[x * nz + zr] = turned[x * share : (x + 1) * share]

    pl.semaphore_wait(barrier, workers - 1 + ny)

    def mech_copy(peer):
        return pltpu.make_async_remote_copy(
            src_ref=mech_out.at[peer], dst_ref=mech_in.at[me], send_sem=mech_ssem, recv_sem=mech_rsem,
            device_id={"sub": peer}, device_id_type=MESH,
        )

    chunk_of_me = me // group

    def slip_copy(peer):
        return pltpu.make_async_remote_copy(
            src_ref=slip_out.at[peer], dst_ref=slip_in.at[me], send_sem=slip_ssem,
            recv_sem=slip_rsem.at[chunk_of_me], device_id={"sub": peer}, device_id_type=MESH,
        )

    @pl.loop(1, workers)
    def _(step):
        mech_copy(peer_of(step)).start()

    pltpu.make_async_copy(mech_out.at[me], mech_in.at[me], mech_rsem).start()

    @pl.loop(1, workers)
    def _(step):
        slip_copy(peer_of(step)).start()

    pltpu.make_async_copy(slip_out.at[me], slip_in.at[me], slip_rsem.at[chunk_of_me]).start()

    def wait_bytes(ref, sem):
        pltpu.make_async_copy(ref, ref, sem).wait()

    get_sgt.wait()
    wait_bytes(mech_in, mech_rsem)
    gathered = mech_in[...].reshape(workers, 128)
    for column in range(12):
        wide[column] = jnp.broadcast_to(gathered[:, column : column + 1], (workers, freqs))

    sites = sgt.shape[4]

    def project(chunk):
        @pl.loop(0, group)
        def _(index):
            worker = chunk * group + index
            blocks = []
            for k in range(2):
                point = table_smem[worker // packs, lax.rem(worker, packs) * 2 + k]
                weights = [
                    jnp.broadcast_to(wide[k * 6 + m, pl.ds(worker, 1), :], (sites, freqs)) for m in range(6)
                ]
                for part_id in range(2):
                    for c in range(2):
                        total = weights[0] * sgt[point, part_id, c, 0].astype(jnp.float32)
                        for m in range(1, 6):
                            total = total + weights[m] * sgt[point, part_id, c, m].astype(jnp.float32)
                        blocks.append(total)
            turned = jnp.concatenate(blocks, axis=0).T
            flip[pl.ds(index, freqs, stride=group), :] = turned

        for x in range(nx):
            rows = share * group
            block = flip[pl.ds(x * rows, rows), :].astype(jnp.bfloat16)
            proj_out[chunk, x] = block.reshape(share, group, 2 * rows_pc)
        for step in range(1, nx):
            proj_copy(chunk, step).start()
        pltpu.make_async_copy(proj_out.at[chunk, my_x], proj_in.at[chunk, my_x], proj_rsem.at[chunk]).start()

    my_z = lax.rem(me, nz)

    def proj_copy(chunk, step):
        x = lax.rem(my_x + step, nx)
        return pltpu.make_async_remote_copy(
            src_ref=proj_out.at[chunk, x], dst_ref=proj_in.at[chunk, my_x], send_sem=proj_ssem.at[chunk],
            recv_sem=proj_rsem.at[chunk], device_id={"sub": x * nz + my_z}, device_id_type=MESH,
        )

    def ring_copy(chunk, step):
        piece = pieces.at[chunk, site]
        return pltpu.make_async_remote_copy(
            src_ref=piece, dst_ref=piece, send_sem=ring_ssem.at[chunk, step - 1],
            recv_sem=ring_rsem.at[chunk, step - 1], device_id={"site": site_of(step)}, device_id_type=MESH,
        )

    def pair_copy(chunk, y):
        piece = pieces.at[chunk, y * 2 + core]
        return pltpu.make_async_remote_copy(
            src_ref=piece, dst_ref=piece, send_sem=pair_ssem.at[chunk], recv_sem=pair_rsem.at[chunk],
            device_id={"site": other}, device_id_type=MESH,
        )

    def share_slip(chunk):
        wait_bytes(slip_in.at[pl.ds(chunk * group, group)], slip_rsem.at[chunk])
        for index in range(group):
            piece_flip[pl.ds(index, share, stride=group), :] = slip_in[chunk * group + index].astype(jnp.float32)
        pieces[chunk, site] = piece_flip[...].astype(jnp.bfloat16).reshape(share, group, vq)
        for step in range(1, ny):
            ring_copy(chunk, step).start()
        pair_copy(chunk, my_y).start()

    for chunk in range(CHUNKS):
        project(chunk)
        share_slip(chunk)
    for chunk in range(CHUNKS):
        for step in range(1, ny):
            y = lax.rem(my_y + ny - step, ny)
            wait_bytes(pieces.at[chunk, y * 2 + core], ring_rsem.at[chunk, step - 1])
            pair_copy(chunk, y).start()
    for chunk in range(CHUNKS):
        wait_bytes(proj_in.at[chunk], proj_rsem.at[chunk])
        wait_bytes(pieces.at[chunk, pl.ds(0, ny)], pair_rsem.at[chunk])

    quads = share // 4
    lane = lax.broadcasted_iota(jnp.int32, (rows_pc // 2, vq), 1)
    even = lane % 2 == 0

    @pl.loop(0, quads)
    def _(quad):
        blocks = []
        for inner in range(4):
            f = quad * 4 + inner
            projected = jnp.concatenate(
                [proj_in[chunk, x, f] for chunk in range(CHUNKS) for x in range(nx)], axis=0
            ).T
            left = jnp.concatenate([projected[:rows_pc], projected[rows_pc:]], axis=1)
            right = jnp.concatenate(
                [pieces[chunk, k * nx + x, f] for k in range(2) for chunk in range(CHUNKS) for x in range(nx)], axis=0
            )
            both = jnp.dot(left, right, preferred_element_type=jnp.float32)
            straight, crossed = both[: rows_pc // 2], both[rows_pc // 2 :]
            swapped = jnp.where(even, -pltpu.roll(crossed, vq - 1, 1), pltpu.roll(crossed, 1, 1))
            blocks.append(straight + swapped)
        part[pl.ds(quad, vq, stride=quads), :] = jnp.concatenate(blocks, axis=0).T

    width = 4 * quads
    part_out[...] = part[...].astype(jnp.bfloat16).reshape(workers, width, 128)

    def part_copy(peer):
        return pltpu.make_async_remote_copy(
            src_ref=part_out.at[peer], dst_ref=part_in.at[me], send_sem=part_ssem, recv_sem=part_rsem,
            device_id={"sub": peer}, device_id_type=MESH,
        )

    @pl.loop(1, workers)
    def _(step):
        part_copy(peer_of(step)).start()

    pltpu.make_async_copy(part_out.at[me], part_in.at[me], part_rsem).start()

    wait_bytes(mech_out.at[pl.ds(0, workers - 1)], mech_ssem)
    wait_bytes(slip_out.at[pl.ds(0, workers - 1)], slip_ssem)
    for chunk in range(CHUNKS):
        wait_bytes(proj_out.at[chunk, pl.ds(0, nx - 1)], proj_ssem.at[chunk])
        for step in range(1, ny):
            wait_bytes(pieces.at[chunk, site], ring_ssem.at[chunk, step - 1])
        wait_bytes(pieces.at[chunk, pl.ds(0, ny)], pair_ssem.at[chunk])
    wait_bytes(part_in, part_rsem)
    wait_bytes(part_out.at[pl.ds(0, workers - 1)], part_ssem)

    totals = []
    for x in range(nx):
        total = part_in[x * nz].astype(jnp.float32)
        for z in range(1, nz):
            total = total + part_in[x * nz + z].astype(jnp.float32)
        totals.append(total)
    for e in range(2):
        for q in range(2):
            start = (e * 2 + q) * quads
            turned = jnp.concatenate([total[start : start + quads] for total in totals], axis=0).T
            rows = rows_pc // 2
            spec_ref[e, q] = jnp.concatenate([turned[i * rows : (i + 1) * rows] for i in range(4)], axis=1)


def spectrum_call(dims, sgt, mechanism, slip, point_list, subfault_counts):
    nx, nz, ny = dims
    workers = nx * nz
    slots, variations, _, freqs = slip.shape
    vq = variations * 2
    rows_pc = 4 * sgt.shape[4]
    share = freqs // nx
    group = workers // CHUNKS
    packs = max(1, min(128 // slots, 2))
    table_rows = workers // packs
    points = point_list.reshape(table_rows, packs * slots)
    width = share
    bf16, f32 = jnp.bfloat16, jnp.float32
    dma = pltpu.SemaphoreType.DMA
    vmem, smem, anywhere = (pl.BlockSpec(memory_space=s) for s in (pltpu.VMEM, pltpu.SMEM, pl.ANY))
    return pl.pallas_call(
        functools.partial(spectrum_kernel, dims),
        out_shape=jax.ShapeDtypeStruct((2, 2, rows_pc // 2, freqs), f32),
        in_specs=[vmem, smem, vmem, anywhere, anywhere],
        out_specs=vmem,
        scratch_shapes=[
            pltpu.VMEM((table_rows + workers, 128), jnp.int32),
            pltpu.SMEM((table_rows + workers, 128), jnp.int32),
            pltpu.VMEM(sgt.shape, bf16),
            pltpu.VMEM((slots, vq, freqs), bf16),
            pltpu.VMEM((workers, 1, 128), f32),
            pltpu.VMEM((workers, 1, 128), f32),
            pltpu.VMEM((12, workers, freqs), f32),
            pltpu.VMEM((workers, share, vq), bf16),
            pltpu.VMEM((workers, share, vq), bf16),
            pltpu.VMEM((freqs * group, 2 * rows_pc), f32),
            pltpu.VMEM((CHUNKS, nx, share, group, 2 * rows_pc), bf16),
            pltpu.VMEM((CHUNKS, nx, share, group, 2 * rows_pc), bf16),
            pltpu.VMEM((CHUNKS, ny * 2, share, group, vq), bf16),
            pltpu.VMEM((share * group, vq), f32),
            pltpu.VMEM((workers * width, 128), f32),
            pltpu.VMEM((workers, width, 128), bf16),
            pltpu.VMEM((workers, width, 128), bf16),
            dma, dma, dma, dma, dma, dma, dma((CHUNKS,)), dma((CHUNKS,)), dma((CHUNKS,)),
            dma((CHUNKS, ny - 1)), dma((CHUNKS, ny - 1)), dma((CHUNKS,)), dma((CHUNKS,)), dma, dma,
        ],
        compiler_params=pltpu.CompilerParams(
            collective_id=0, has_side_effects=True, vmem_limit_bytes=63 * 1024 * 1024
        ),
        name="spectrum",
    )(points, subfault_counts, mechanism.T, slip.reshape(slots, vq, freqs), sgt)


def synthesis_kernel(spec_ref, gain_ref, high_ref, low_ref, seis_ref, psa_ref, response, source, peak):
    step = pl.program_id(0)
    periods = gain_ref.shape[1]
    freqs = gain_ref.shape[2]
    rows = source.shape[1]

    @pl.when(step == 0)
    def _():
        real = jnp.concatenate([spec_ref[0, 0], spec_ref[1, 0]], axis=0)
        imag = jnp.concatenate([spec_ref[0, 1], spec_ref[1, 1]], axis=0)
        spectrum = jnp.concatenate([real, imag], axis=1)
        top = spectrum.astype(jnp.bfloat16)
        source[0] = top
        source[1] = (spectrum - top.astype(jnp.float32)).astype(jnp.bfloat16)
        for q in range(periods):
            g0 = gain_ref[0, q : q + 1, :]
            g1 = gain_ref[1, q : q + 1, :]
            response[pl.ds(q * rows, rows), pl.ds(0, freqs)] = (g0 * real - g1 * imag).astype(jnp.bfloat16)
            response[pl.ds(q * rows, rows), pl.ds(freqs, freqs)] = (g0 * imag + g1 * real).astype(jnp.bfloat16)
        peak[...] = jnp.zeros_like(peak)

    high = high_ref[...]
    motion = (
        jnp.dot(source[0], high, preferred_element_type=jnp.float32)
        + jnp.dot(source[1], high, preferred_element_type=jnp.float32)
        + jnp.dot(source[0], low_ref[...], preferred_element_type=jnp.float32)
    )
    seis_ref[...] = motion.astype(jnp.bfloat16)
    per = 8
    for start in range(0, periods, per):
        part = pl.ds(start * rows, per * rows)
        wave = jnp.abs(jnp.dot(response[part, :], high, preferred_element_type=jnp.float32))
        most = peak[part, :]
        for t in range(0, wave.shape[1], 128):
            most = jnp.maximum(most, wave[:, t : t + 128])
        peak[part, :] = most

    @pl.when(step == pl.num_programs(0) - 1)
    def _():
        lane = lax.broadcasted_iota(jnp.int32, (rows, periods), 1)
        total = jnp.zeros((rows, periods), jnp.float32)
        for q in range(periods):
            most = jnp.max(peak[pl.ds(q * rows, rows), :], axis=1, keepdims=True)
            total = jnp.where(lane == q, most, total)
        psa_ref[...] = total


def synthesis_call(spec):
    rows, freqs = 2 * spec.shape[2], spec.shape[3]
    high, low = synthesis_basis(freqs, NT)
    gains = oscillator_gains(PERIODS, freqs, NT)
    tile = 256
    return pl.pallas_call(
        synthesis_kernel,
        grid=(NT // tile,),
        out_shape=(
            jax.ShapeDtypeStruct((rows, NT), jnp.bfloat16),
            jax.ShapeDtypeStruct((rows, PERIODS), jnp.float32),
        ),
        in_specs=[
            pl.BlockSpec(spec.shape, lambda t: (0, 0, 0, 0)),
            pl.BlockSpec(gains.shape, lambda t: (0, 0, 0)),
            pl.BlockSpec((2 * freqs, tile), lambda t: (0, t)),
            pl.BlockSpec((2 * freqs, tile), lambda t: (0, t)),
        ],
        out_specs=(
            pl.BlockSpec((rows, tile), lambda t: (0, t)),
            pl.BlockSpec((rows, PERIODS), lambda t: (0, 0)),
        ),
        scratch_shapes=[
            pltpu.VMEM((PERIODS * rows, 2 * freqs), jnp.bfloat16),
            pltpu.VMEM((2, rows, 2 * freqs), jnp.bfloat16),
            pltpu.VMEM((PERIODS * rows, 128), jnp.float32),
        ],
        compiler_params=pltpu.CompilerParams(dimension_semantics=("arbitrary",)),
        name="synthesis",
    )(spec, jnp.asarray(gains), jnp.asarray(high), jnp.asarray(low))


def per_device(dims, sgt, mechanism, slip, point_list, subfault_counts):
    spec = spectrum_call(dims, sgt, mechanism, slip, point_list, subfault_counts)
    seis, psa = synthesis_call(spec)
    sites = sgt.shape[4]
    return seis.reshape(2, 2, sites, NT), psa.reshape(2, 2, sites, PERIODS)


def solution(mesh):
    workers, site_devices = mesh.shape["sub"], mesh.shape["site"]
    nx = site_devices // 2
    dims = (nx, workers // nx, site_devices // 2)
    in_specs = (
        P("sub", None, None, None, "site", None),
        P("sub", None),
        P("sub", None, None, None),
        P(),
        P(),
    )
    out_specs = (P("sub", None, "site", None), P("sub", None, "site", None))
    return jax.shard_map(
        functools.partial(per_device, dims), mesh=mesh, in_specs=in_specs, out_specs=out_specs, check_vma=False
    )
```

```python
import functools
import math

import jax
import jax.numpy as jnp
import numpy as np
from jax import lax
from jax.experimental import pallas as pl
from jax.experimental.pallas import tpu as pltpu
from jax.sharding import PartitionSpec as P

NT = 2048
PERIODS = 40
HALVES = 2
CUTS = 4
MESH = pl.DeviceIdType.MESH

damping = 0.05
sample_step = 0.1


def bins_in_order(freq_count):
    kappa = np.arange(freq_count)
    quarter = freq_count // 4
    return 4 * (kappa % quarter) + kappa // quarter


def synthesis_basis(freq_count, sample_count):
    freq_ids = bins_in_order(freq_count)
    angles = (freq_ids[:, None] * np.arange(sample_count)[None, :] % sample_count) * (2.0 * math.pi / sample_count)
    scale = 1.0 / math.sqrt(freq_count)
    both = np.concatenate([scale * np.cos(angles), -scale * np.sin(angles)], axis=0).astype(np.float32)
    high = both.astype(jnp.bfloat16)
    low = (both - high.astype(np.float32)).astype(jnp.bfloat16)
    return high, low


def oscillator_gains(period_count, freq_count, sample_count):
    periods = 2.0 * np.exp(np.arange(period_count) * (math.log(5.0) / max(period_count - 1, 1)))
    natural = 2.0 * math.pi / periods
    omega = bins_in_order(freq_count) * (2.0 * math.pi / (sample_count * sample_step))
    squared = (natural * natural)[:, None]
    real_part = squared - (omega * omega)[None, :]
    imag_part = 2.0 * damping * natural[:, None] * omega[None, :]
    magnitude = real_part * real_part + imag_part * imag_part
    return np.stack([-squared * real_part / magnitude, squared * imag_part / magnitude]).astype(np.float32)


def spectrum_kernel(
    dims, points_ref, counts_ref, mech_ref, slip_hbm, sgt_hbm, spec_ref,
    table, table_smem, sgt, slip, mech_out, mech_in, wide, slip_out, slip_in, flip, near_out, near_in, far_out, far_in,
    pieces, piece_flip, part, part_out, part_in, sums,
    table_sem, sgt_sem, slip_sem, mech_ssem, mech_rsem, slip_ssem, slip_rsem, near_ssem, near_rsem, far_ssem, far_rsem,
    ring_ssem, ring_rsem, pair_ssem, pair_rsem, part_ssem, part_rsem,
):
    nx, nz, ny = dims
    workers = nx * nz
    slots, vq, freqs = slip.shape
    sites = sgt.shape[4]
    rows_pc = 4 * sites
    per_reader = sgt.shape[0]
    share = freqs // nx
    group = workers // 2
    packs = points_ref.shape[1] // slots
    table_rows = points_ref.shape[0]
    lanes = points_ref.shape[1]
    halves = slip_out.shape[0]
    half = share // halves
    cuts = far_out.shape[0]
    cut = share // cuts
    quads = cut // 4

    me = lax.axis_index("sub")
    site = lax.axis_index("site")
    my_x = me // nz
    my_z = lax.rem(me, nz)
    my_y = site // 2
    core = lax.rem(site, 2)
    other = my_y * 2 + (1 - core)

    get_slip = pltpu.make_async_copy(slip_hbm, slip, slip_sem)
    get_slip.start()
    get_sgt = pltpu.make_async_copy(sgt_hbm, sgt, sgt_sem)
    get_sgt.start()

    def each_peer(act):
        xs = [lax.rem(my_x + dx, nx) for dx in range(nx)]
        order = sorted(range(nx), key=lambda dx: -min(dx, nx - dx))

        @pl.loop(0, nz - 1)
        def _(step):
            away = (step + 1) // 2
            dz = nz // 2 + jnp.where(lax.rem(step, 2) == 0, away, -away)
            z = lax.rem(my_z + dz, nz)
            place = lax.rem(nz - dz + 1, nz) * nx + my_x
            for dx in order:
                act(xs[dx], z, place)

        for dx in order:
            if dx:
                act(xs[dx], my_z, nx + my_x)

    my_place = nx + my_x

    def site_of(step):
        return lax.rem(my_y + step, ny) * 2 + core

    barrier = pltpu.get_barrier_semaphore()

    def greet(x, z, place):
        pl.semaphore_signal(barrier, inc=1, device_id={"sub": x * nz + z}, device_id_type=MESH)

    each_peer(greet)
    for step in range(1, ny):
        pl.semaphore_signal(barrier, inc=1, device_id={"site": site_of(step)}, device_id_type=MESH)
    pl.semaphore_signal(barrier, inc=1, device_id={"site": other}, device_id_type=MESH)

    points = points_ref[...]
    lane = lax.broadcasted_iota(jnp.int32, (table_rows, lanes), 1)
    out_lane = lax.broadcasted_iota(jnp.int32, (table_rows, 128), 1)
    mine = points // per_reader == me
    local = points % per_reader
    named = jnp.zeros((table_rows, 128), jnp.int32)
    for pack in range(packs):
        here = mine & (lane // slots == pack)
        first = jnp.min(jnp.where(here, lane, lanes), axis=1, keepdims=True)
        last = jnp.max(jnp.where(here, lane, -1), axis=1, keepdims=True)
        for k, found in enumerate((first, last)):
            row = jnp.sum(jnp.where(here & (lane == found), local, 0), axis=1, keepdims=True)
            named = jnp.where(out_lane == pack * 2 + k, row, named)
    table[pl.ds(0, table_rows), :] = named

    my_points = points_ref[pl.ds(me // packs, 1), :]
    lane = lax.broadcasted_iota(jnp.int32, (workers, lanes), 1)
    out_lane = lax.broadcasted_iota(jnp.int32, (workers, 128), 1)
    reader = lax.broadcasted_iota(jnp.int32, (workers, lanes), 0)
    base = lax.rem(me, packs) * slots
    here = (my_points // per_reader == reader) & (lane >= base) & (lane < base + slots)
    first = jnp.min(jnp.where(here, lane, lanes), axis=1, keepdims=True)
    last = jnp.max(jnp.where(here, lane, -1), axis=1, keepdims=True)
    table[pl.ds(table_rows, workers), :] = jnp.clip(jnp.where(out_lane == 0, first, last) - base, 0, slots - 1)
    to_smem = pltpu.make_async_copy(table, table_smem, table_sem)
    to_smem.start()

    live = lane - base < counts_ref[me]
    moments = jnp.concatenate([mech_ref[...]] * packs, axis=1)
    sent = jnp.zeros((workers, 128), jnp.float32)
    for k, found in enumerate((first, last)):
        chosen = here & live & (lane == found)
        for m in range(6):
            value = jnp.sum(jnp.where(chosen, moments[m : m + 1, :], 0.0), axis=1, keepdims=True)
            sent = jnp.where(out_lane == k * 6 + m, value, sent)
    mech_out[...] = sent.reshape(workers, 1, 128)

    to_smem.wait()
    get_slip.wait()
    my_k = site // nx
    x_of_piece = lax.rem(site, nx)

    @pl.loop(0, nz)
    def _(zr):
        slot = table_smem[table_rows + x_of_piece * nz + zr, my_k]
        turned = slip[slot].astype(jnp.float32).T.astype(jnp.bfloat16)
        for h in range(halves):
            for x in range(nx):
                start = x * share + h * half
                slip_out[h, x * nz + zr] = turned[start : start + half]

    get_sgt.wait()
    pl.semaphore_wait(barrier, workers - 1 + ny)

    def wait_bytes(ref, sem):
        pltpu.make_async_copy(ref, ref, sem).wait()

    def send_mech(x, z, place):
        pltpu.make_async_remote_copy(
            src_ref=mech_out.at[x * nz + z], dst_ref=mech_in.at[place], send_sem=mech_ssem,
            recv_sem=mech_rsem.at[place // group], device_id={"sub": x * nz + z}, device_id_type=MESH,
        ).start()

    each_peer(send_mech)
    pltpu.make_async_copy(mech_out.at[me], mech_in.at[my_place], mech_rsem.at[my_place // group]).start()

    for h in range(halves):

        def send_slip(x, z, place, h=h):
            pltpu.make_async_remote_copy(
                src_ref=slip_out.at[h, x * nz + z], dst_ref=slip_in.at[h, place], send_sem=slip_ssem,
                recv_sem=slip_rsem.at[h], device_id={"sub": x * nz + z}, device_id_type=MESH,
            ).start()

        each_peer(send_slip)
        pltpu.make_async_copy(slip_out.at[h, me], slip_in.at[h, my_place], slip_rsem.at[h]).start()

    def project(turn):
        wait_bytes(mech_in.at[pl.ds(turn * group, group)], mech_rsem.at[turn])
        gathered = mech_in[pl.ds(turn * group, group)].reshape(group, 128)
        for column in range(12):
            wide[column] = jnp.broadcast_to(gathered[:, column : column + 1], (group, freqs))

        @pl.loop(0, group, unroll=2)
        def _(index):
            place = turn * group + index
            worker = lax.rem(place, nx) * nz + lax.rem(my_z + place // nx + nz - 1, nz)
            blocks = []
            for k in range(2):
                point = table_smem[worker // packs, lax.rem(worker, packs) * 2 + k]
                weights = [
                    jnp.broadcast_to(wide[k * 6 + m, pl.ds(index, 1), :], (sites, freqs)) for m in range(6)
                ]
                for part_id in range(2):
                    for c in range(2):
                        total = weights[0] * sgt[point, part_id, c, 0].astype(jnp.float32)
                        for m in range(1, 6):
                            total = total + weights[m] * sgt[point, part_id, c, m].astype(jnp.float32)
                        blocks.append(total)
            turned = jnp.concatenate(blocks, axis=0).T
            flip[pl.ds(index, freqs, stride=group), :] = turned

    def near_copy(step):
        x = lax.rem(my_x + step, nx)
        return pltpu.make_async_remote_copy(
            src_ref=near_out.at[x], dst_ref=near_in.at[my_x], send_sem=near_ssem, recv_sem=near_rsem,
            device_id={"sub": x * nz + my_z}, device_id_type=MESH,
        )

    def far_copy(i, step):
        x = lax.rem(my_x + step, nx)
        return pltpu.make_async_remote_copy(
            src_ref=far_out.at[i, x], dst_ref=far_in.at[i, my_x], send_sem=far_ssem.at[i],
            recv_sem=far_rsem.at[i], device_id={"sub": x * nz + my_z}, device_id_type=MESH,
        )

    def ring_copy(h, step):
        piece = pieces.at[h, site]
        return pltpu.make_async_remote_copy(
            src_ref=piece, dst_ref=piece, send_sem=ring_ssem.at[h, step - 1],
            recv_sem=ring_rsem.at[h, step - 1], device_id={"site": site_of(step)}, device_id_type=MESH,
        )

    def pair_copy(h, y):
        piece = pieces.at[h, y * 2 + core]
        return pltpu.make_async_remote_copy(
            src_ref=piece, dst_ref=piece, send_sem=pair_ssem.at[h], recv_sem=pair_rsem.at[h],
            device_id={"site": other}, device_id_type=MESH,
        )

    hops = sorted(range(1, nx), key=lambda dx: -min(dx, nx - dx))

    def send_near():
        for x in range(nx):
            rows = share * group
            near_out[x] = flip[pl.ds(x * rows, rows), :].astype(jnp.bfloat16).reshape(share, group, 2 * rows_pc)
        for step in hops:
            near_copy(step).start()
        pltpu.make_async_copy(near_out.at[my_x], near_in.at[my_x], near_rsem).start()

    def send_far():
        for i in range(cuts):
            for x in range(nx):
                rows = cut * group
                block = flip[pl.ds((x * cuts + i) * rows, rows), :].astype(jnp.bfloat16)
                far_out[i, x] = block.reshape(cut, group, 2 * rows_pc)
            for step in hops:
                far_copy(i, step).start()
            pltpu.make_async_copy(far_out.at[i, my_x], far_in.at[i, my_x], far_rsem.at[i]).start()

    def share_slip(h):
        wait_bytes(slip_in.at[h], slip_rsem.at[h])
        for place in range(workers):
            piece_flip[pl.ds(place, half, stride=workers), :] = slip_in[h, place].astype(jnp.float32)
        pieces[h, site] = piece_flip[...].astype(jnp.bfloat16).reshape(half, workers, vq)
        for step in range(1, ny):
            ring_copy(h, step).start()
        pair_copy(h, my_y).start()

    def pass_on(h):
        for step in range(1, ny):
            y = lax.rem(my_y + ny - step, ny)
            wait_bytes(pieces.at[h, y * 2 + core], ring_rsem.at[h, step - 1])
            pair_copy(h, y).start()

    lane = lax.broadcasted_iota(jnp.int32, (rows_pc // 2, vq), 1)
    even = lane % 2 == 0

    def contract(i):
        wait_bytes(far_in.at[i], far_rsem.at[i])
        for quad in range(quads):
            blocks = []
            for inner in range(4):
                f = quad * 4 + inner
                whole = i * cut + f
                projected = jnp.concatenate(
                    [near_in[x, whole] for x in range(nx)] + [far_in[i, x, f] for x in range(nx)], axis=0
                ).T
                left = jnp.concatenate([projected[:rows_pc], projected[rows_pc:]], axis=1)
                right = jnp.concatenate(
                    [
                        pieces[whole // half, k * nx + x, whole % half, pl.ds(turn * group, group), :]
                        for k in range(2)
                        for turn in range(2)
                        for x in range(nx)
                    ],
                    axis=0,
                )
                both = jnp.dot(left, right, preferred_element_type=jnp.float32)
                straight, crossed = both[: rows_pc // 2], both[rows_pc // 2 :]
                swapped = jnp.where(even, -pltpu.roll(crossed, vq - 1, 1), pltpu.roll(crossed, 1, 1))
                blocks.append(straight + swapped)
            part[i, pl.ds(quad, vq, stride=quads), :] = jnp.concatenate(blocks, axis=0).T
        part_out[i] = part[i].astype(jnp.bfloat16).reshape(workers, 4 * quads, 128)

        def send_part(x, z, place):
            pltpu.make_async_remote_copy(
                src_ref=part_out.at[i, x * nz + z], dst_ref=part_in.at[i, me], send_sem=part_ssem,
                recv_sem=part_rsem.at[i], device_id={"sub": x * nz + z}, device_id_type=MESH,
            ).start()

        each_peer(send_part)
        pltpu.make_async_copy(part_out.at[i, me], part_in.at[i, me], part_rsem.at[i]).start()

    project(0)
    send_near()
    share_slip(0)
    project(1)
    send_far()
    for h in range(1, halves):
        share_slip(h)
    pass_on(0)
    wait_bytes(near_in, near_rsem)
    for i in range(cuts):
        if i % (cuts // halves) == 0:
            h = i // (cuts // halves)
            if h:
                pass_on(h)
            wait_bytes(pieces.at[h, pl.ds(0, ny)], pair_rsem.at[h])
        contract(i)

    wait_bytes(mech_out.at[pl.ds(0, workers - 1)], mech_ssem)
    wait_bytes(slip_out.at[:, pl.ds(0, workers - 1)], slip_ssem)
    wait_bytes(near_out.at[pl.ds(0, nx - 1)], near_ssem)
    for i in range(cuts):
        wait_bytes(far_out.at[i, pl.ds(0, nx - 1)], far_ssem.at[i])
    for h in range(halves):
        for step in range(1, ny):
            wait_bytes(pieces.at[h, site], ring_ssem.at[h, step - 1])
        wait_bytes(pieces.at[h, pl.ds(0, ny)], pair_ssem.at[h])

    for i in range(cuts):
        wait_bytes(part_in.at[i], part_rsem.at[i])
        for x in range(nx):
            total = part_in[i, x * nz].astype(jnp.float32)
            for z in range(1, nz):
                total = total + part_in[i, x * nz + z].astype(jnp.float32)
            for row in range(4):
                sums[row, pl.ds((x * cuts + i) * quads, quads), :] = total[row * quads : (row + 1) * quads]
    rows = rows_pc // 2
    for e in range(2):
        for q in range(2):
            turned = sums[e * 2 + q].T
            spec_ref[e, q] = jnp.concatenate([turned[i * rows : (i + 1) * rows] for i in range(4)], axis=1)
    wait_bytes(part_out.at[:, pl.ds(0, workers - 1)], part_ssem)


def spectrum_call(dims, sgt, mechanism, slip, point_list, subfault_counts):
    nx, nz, ny = dims
    workers = nx * nz
    slots, variations, _, freqs = slip.shape
    vq = variations * 2
    rows_pc = 4 * sgt.shape[4]
    share = freqs // nx
    group = workers // 2
    half, cut = share // HALVES, share // CUTS
    quads = cut // 4
    packs = max(1, min(128 // slots, 2))
    table_rows = workers // packs
    points = point_list.reshape(table_rows, packs * slots)
    bf16, f32 = jnp.bfloat16, jnp.float32
    dma = pltpu.SemaphoreType.DMA
    vmem, smem, anywhere = (pl.BlockSpec(memory_space=s) for s in (pltpu.VMEM, pltpu.SMEM, pl.ANY))
    return pl.pallas_call(
        functools.partial(spectrum_kernel, dims),
        out_shape=jax.ShapeDtypeStruct((2, 2, rows_pc // 2, freqs), f32),
        in_specs=[vmem, smem, vmem, anywhere, anywhere],
        out_specs=vmem,
        scratch_shapes=[
            pltpu.VMEM((table_rows + workers, 128), jnp.int32),
            pltpu.SMEM((table_rows + workers, 128), jnp.int32),
            pltpu.VMEM(sgt.shape, bf16),
            pltpu.VMEM((slots, vq, freqs), bf16),
            pltpu.VMEM((workers, 1, 128), f32),
            pltpu.VMEM((workers, 1, 128), f32),
            pltpu.VMEM((12, group, freqs), f32),
            pltpu.VMEM((HALVES, workers, half, vq), bf16),
            pltpu.VMEM((HALVES, workers, half, vq), bf16),
            pltpu.VMEM((freqs * group, 2 * rows_pc), f32),
            pltpu.VMEM((nx, share, group, 2 * rows_pc), bf16),
            pltpu.VMEM((nx, share, group, 2 * rows_pc), bf16),
            pltpu.VMEM((CUTS, nx, cut, group, 2 * rows_pc), bf16),
            pltpu.VMEM((CUTS, nx, cut, group, 2 * rows_pc), bf16),
            pltpu.VMEM((HALVES, ny * 2, half, workers, vq), bf16),
            pltpu.VMEM((half * workers, vq), f32),
            pltpu.VMEM((CUTS, vq * quads, 128), f32),
            pltpu.VMEM((CUTS, workers, 4 * quads, 128), bf16),
            pltpu.VMEM((CUTS, workers, 4 * quads, 128), bf16),
            pltpu.VMEM((4, share // 4 * nx, 128), f32),
            dma, dma, dma, dma, dma((2,)), dma, dma((HALVES,)), dma, dma, dma((CUTS,)), dma((CUTS,)),
            dma((HALVES, ny - 1)), dma((HALVES, ny - 1)), dma((HALVES,)), dma((HALVES,)), dma, dma((CUTS,)),
        ],
        compiler_params=pltpu.CompilerParams(
            collective_id=0, has_side_effects=True, vmem_limit_bytes=63 * 1024 * 1024
        ),
        name="spectrum",
    )(points, subfault_counts, mechanism.T, slip.reshape(slots, vq, freqs), sgt)


def synthesis_kernel(spec_ref, gain_ref, high_ref, low_ref, seis_ref, psa_ref, response, source, peak):
    step = pl.program_id(0)
    periods = gain_ref.shape[1]
    freqs = gain_ref.shape[2]
    rows = source.shape[1]

    @pl.when(step == 0)
    def _():
        real = jnp.concatenate([spec_ref[0, 0], spec_ref[1, 0]], axis=0)
        imag = jnp.concatenate([spec_ref[0, 1], spec_ref[1, 1]], axis=0)
        spectrum = jnp.concatenate([real, imag], axis=1)
        top = spectrum.astype(jnp.bfloat16)
        source[0] = top
        source[1] = (spectrum - top.astype(jnp.float32)).astype(jnp.bfloat16)
        for q in range(periods):
            g0 = gain_ref[0, q : q + 1, :]
            g1 = gain_ref[1, q : q + 1, :]
            response[pl.ds(q * rows, rows), pl.ds(0, freqs)] = (g0 * real - g1 * imag).astype(jnp.bfloat16)
            response[pl.ds(q * rows, rows), pl.ds(freqs, freqs)] = (g0 * imag + g1 * real).astype(jnp.bfloat16)
        peak[...] = jnp.zeros_like(peak)

    high = high_ref[...]
    motion = (
        jnp.dot(source[0], high, preferred_element_type=jnp.float32)
        + jnp.dot(source[1], high, preferred_element_type=jnp.float32)
        + jnp.dot(source[0], low_ref[...], preferred_element_type=jnp.float32)
    )
    seis_ref[...] = motion.astype(jnp.bfloat16)
    per = 8
    for start in range(0, periods, per):
        part = pl.ds(start * rows, per * rows)
        wave = jnp.abs(jnp.dot(response[part, :], high, preferred_element_type=jnp.float32))
        most = peak[part, :]
        for t in range(0, wave.shape[1], 128):
            most = jnp.maximum(most, wave[:, t : t + 128])
        peak[part, :] = most

    @pl.when(step == pl.num_programs(0) - 1)
    def _():
        lane = lax.broadcasted_iota(jnp.int32, (rows, periods), 1)
        total = jnp.zeros((rows, periods), jnp.float32)
        for q in range(periods):
            most = jnp.max(peak[pl.ds(q * rows, rows), :], axis=1, keepdims=True)
            total = jnp.where(lane == q, most, total)
        psa_ref[...] = total


def synthesis_call(spec):
    rows, freqs = 2 * spec.shape[2], spec.shape[3]
    high, low = synthesis_basis(freqs, NT)
    gains = oscillator_gains(PERIODS, freqs, NT)
    tile = 256
    return pl.pallas_call(
        synthesis_kernel,
        grid=(NT // tile,),
        out_shape=(
            jax.ShapeDtypeStruct((rows, NT), jnp.bfloat16),
            jax.ShapeDtypeStruct((rows, PERIODS), jnp.float32),
        ),
        in_specs=[
            pl.BlockSpec(spec.shape, lambda t: (0, 0, 0, 0)),
            pl.BlockSpec(gains.shape, lambda t: (0, 0, 0)),
            pl.BlockSpec((2 * freqs, tile), lambda t: (0, t)),
            pl.BlockSpec((2 * freqs, tile), lambda t: (0, t)),
        ],
        out_specs=(
            pl.BlockSpec((rows, tile), lambda t: (0, t)),
            pl.BlockSpec((rows, PERIODS), lambda t: (0, 0)),
        ),
        scratch_shapes=[
            pltpu.VMEM((PERIODS * rows, 2 * freqs), jnp.bfloat16),
            pltpu.VMEM((2, rows, 2 * freqs), jnp.bfloat16),
            pltpu.VMEM((PERIODS * rows, 128), jnp.float32),
        ],
        compiler_params=pltpu.CompilerParams(dimension_semantics=("arbitrary",)),
        name="synthesis",
    )(spec, jnp.asarray(gains), jnp.asarray(high), jnp.asarray(low))


def per_device(dims, sgt, mechanism, slip, point_list, subfault_counts):
    spec = spectrum_call(dims, sgt, mechanism, slip, point_list, subfault_counts)
    seis, psa = synthesis_call(spec)
    sites = sgt.shape[4]
    return seis.reshape(2, 2, sites, NT), psa.reshape(2, 2, sites, PERIODS)


def solution(mesh):
    workers, site_devices = mesh.shape["sub"], mesh.shape["site"]
    nx = site_devices // 2
    dims = (nx, workers // nx, site_devices // 2)
    in_specs = (
        P("sub", None, None, None, "site", None),
        P("sub", None),
        P("sub", None, None, None),
        P(),
        P(),
    )
    out_specs = (P("sub", None, "site", None), P("sub", None, "site", None))
    return jax.shard_map(
        functools.partial(per_device, dims), mesh=mesh, in_specs=in_specs, out_specs=out_specs, check_vma=False
    )
```

```python
import functools
import math

import jax
import jax.numpy as jnp
import numpy as np
from jax import lax
from jax.experimental import pallas as pl
from jax.experimental.pallas import tpu as pltpu
from jax.sharding import PartitionSpec as P

NT = 2048
PERIODS = 40
HALVES = 2
CUTS = 4
PARTS = 5
TILE = 512
MESH = pl.DeviceIdType.MESH

damping = 0.05
sample_step = 0.1


def bins_in_order(freq_count):
    kappa = np.arange(freq_count)
    quarter = freq_count // 4
    return 4 * (kappa % quarter) + kappa // quarter


def synthesis_basis(freq_count, sample_count):
    freq_ids = bins_in_order(freq_count)
    angles = (freq_ids[:, None] * np.arange(sample_count)[None, :] % sample_count) * (2.0 * math.pi / sample_count)
    scale = 1.0 / math.sqrt(freq_count)
    both = np.concatenate([scale * np.cos(angles), -scale * np.sin(angles)], axis=0).astype(np.float32)
    high = both.astype(jnp.bfloat16)
    low = (both - high.astype(np.float32)).astype(jnp.bfloat16)
    return high, low


def oscillator_gains(period_count, freq_count, sample_count):
    periods = 2.0 * np.exp(np.arange(period_count) * (math.log(5.0) / max(period_count - 1, 1)))
    natural = 2.0 * math.pi / periods
    omega = bins_in_order(freq_count) * (2.0 * math.pi / (sample_count * sample_step))
    squared = (natural * natural)[:, None]
    real_part = squared - (omega * omega)[None, :]
    imag_part = 2.0 * damping * natural[:, None] * omega[None, :]
    magnitude = real_part * real_part + imag_part * imag_part
    return np.stack([-squared * real_part / magnitude, squared * imag_part / magnitude]).astype(np.float32)


def spectrum_kernel(
    dims, points_hbm, counts_hbm, mech_hbm, slip_hbm, sgt_hbm, spec_ref,
    points_ref, counts_ref, mech_ref, table, table_smem, sgt, slip, mech_out, mech_in, wide, slip_out, slip_in, flip, near_out, near_in, far_out, far_in,
    pieces, piece_flip, part, part_out, part_in, sums,
    small_sem, table_sem, sgt_sem, slip_sem, mech_ssem, mech_rsem, slip_ssem, slip_rsem, near_ssem, near_rsem, far_ssem, far_rsem,
    ring_ssem, ring_rsem, pair_ssem, pair_rsem, part_ssem, part_rsem,
):
    nx, nz, ny = dims
    workers = nx * nz
    slots, vq, freqs = slip.shape
    sites = sgt.shape[4]
    rows_pc = 4 * sites
    per_reader = sgt.shape[0]
    share = freqs // nx
    group = workers // 2
    packs = points_ref.shape[1] // slots
    table_rows = points_ref.shape[0]
    lanes = points_ref.shape[1]
    halves = slip_out.shape[0]
    half = share // halves
    cuts = far_out.shape[0]
    cut = share // cuts
    quads = cut // 4

    me = lax.axis_index("sub")
    site = lax.axis_index("site")
    my_x = me // nz
    my_z = lax.rem(me, nz)
    my_y = site // 2
    core = lax.rem(site, 2)
    other = my_y * 2 + (1 - core)

    small = [
        pltpu.make_async_copy(source, target, small_sem.at[i])
        for i, (source, target) in enumerate(
            ((points_hbm, points_ref), (counts_hbm, counts_ref), (mech_hbm, mech_ref))
        )
    ]
    for copy in small:
        copy.start()
    get_slip = pltpu.make_async_copy(slip_hbm, slip, slip_sem)
    get_slip.start()
    get_sgt = pltpu.make_async_copy(sgt_hbm, sgt, sgt_sem)
    get_sgt.start()

    def each_peer(act):
        xs = [lax.rem(my_x + dx, nx) for dx in range(nx)]
        order = sorted(range(nx), key=lambda dx: -min(dx, nx - dx))

        @pl.loop(0, nz - 1)
        def _(step):
            away = (step + 1) // 2
            dz = nz // 2 + jnp.where(lax.rem(step, 2) == 0, away, -away)
            z = lax.rem(my_z + dz, nz)
            place = lax.rem(nz - dz + 1, nz) * nx + my_x
            for dx in order:
                act(xs[dx], z, place)

        for dx in order:
            if dx:
                act(xs[dx], my_z, nx + my_x)

    my_place = nx + my_x

    def site_of(step):
        return lax.rem(my_y + step, ny) * 2 + core

    barrier = pltpu.get_barrier_semaphore()

    def greet(x, z, place):
        pl.semaphore_signal(barrier, inc=1, device_id={"sub": x * nz + z}, device_id_type=MESH)

    each_peer(greet)
    for step in range(1, ny):
        pl.semaphore_signal(barrier, inc=1, device_id={"site": site_of(step)}, device_id_type=MESH)
    pl.semaphore_signal(barrier, inc=1, device_id={"site": other}, device_id_type=MESH)

    for copy in small:
        copy.wait()
    points = points_ref[...]
    lane = lax.broadcasted_iota(jnp.int32, (table_rows, lanes), 1)
    out_lane = lax.broadcasted_iota(jnp.int32, (table_rows, 128), 1)
    mine = points // per_reader == me
    local = points % per_reader
    named = jnp.zeros((table_rows, 128), jnp.int32)
    for pack in range(packs):
        here = mine & (lane // slots == pack)
        first = jnp.min(jnp.where(here, lane, lanes), axis=1, keepdims=True)
        last = jnp.max(jnp.where(here, lane, -1), axis=1, keepdims=True)
        for k, found in enumerate((first, last)):
            row = jnp.sum(jnp.where(here & (lane == found), local, 0), axis=1, keepdims=True)
            named = jnp.where(out_lane == pack * 2 + k, row, named)
    table[pl.ds(0, table_rows), :] = named

    my_points = points_ref[pl.ds(me // packs, 1), :]
    lane = lax.broadcasted_iota(jnp.int32, (workers, lanes), 1)
    out_lane = lax.broadcasted_iota(jnp.int32, (workers, 128), 1)
    reader = lax.broadcasted_iota(jnp.int32, (workers, lanes), 0)
    base = lax.rem(me, packs) * slots
    here = (my_points // per_reader == reader) & (lane >= base) & (lane < base + slots)
    first = jnp.min(jnp.where(here, lane, lanes), axis=1, keepdims=True)
    last = jnp.max(jnp.where(here, lane, -1), axis=1, keepdims=True)
    table[pl.ds(table_rows, workers), :] = jnp.clip(jnp.where(out_lane == 0, first, last) - base, 0, slots - 1)
    to_smem = pltpu.make_async_copy(table, table_smem, table_sem)
    to_smem.start()

    live = lane - base < counts_ref[me]
    moments = jnp.concatenate([mech_ref[...]] * packs, axis=1)
    sent = jnp.zeros((workers, 128), jnp.float32)
    for k, found in enumerate((first, last)):
        chosen = here & live & (lane == found)
        for m in range(6):
            value = jnp.sum(jnp.where(chosen, moments[m : m + 1, :], 0.0), axis=1, keepdims=True)
            sent = jnp.where(out_lane == k * 6 + m, value, sent)
    mech_out[...] = sent.reshape(workers, 1, 128)

    to_smem.wait()
    get_slip.wait()
    my_k = site // nx
    x_of_piece = lax.rem(site, nx)

    @pl.loop(0, nz)
    def _(zr):
        slot = table_smem[table_rows + x_of_piece * nz + zr, my_k]
        turned = slip[slot].astype(jnp.float32).T.astype(jnp.bfloat16)
        for h in range(halves):
            for x in range(nx):
                start = x * share + h * half
                slip_out[h, x * nz + zr] = turned[start : start + half]

    get_sgt.wait()
    pl.semaphore_wait(barrier, workers - 1 + ny)

    def wait_bytes(ref, sem):
        pltpu.make_async_copy(ref, ref, sem).wait()

    def send_mech(x, z, place):
        pltpu.make_async_remote_copy(
            src_ref=mech_out.at[x * nz + z], dst_ref=mech_in.at[place], send_sem=mech_ssem,
            recv_sem=mech_rsem.at[place // group], device_id={"sub": x * nz + z}, device_id_type=MESH,
        ).start()

    each_peer(send_mech)
    pltpu.make_async_copy(mech_out.at[me], mech_in.at[my_place], mech_rsem.at[my_place // group]).start()

    for h in range(halves):

        def send_slip(x, z, place, h=h):
            pltpu.make_async_remote_copy(
                src_ref=slip_out.at[h, x * nz + z], dst_ref=slip_in.at[h, place], send_sem=slip_ssem,
                recv_sem=slip_rsem.at[h], device_id={"sub": x * nz + z}, device_id_type=MESH,
            ).start()

        each_peer(send_slip)
        pltpu.make_async_copy(slip_out.at[h, me], slip_in.at[h, my_place], slip_rsem.at[h]).start()

    def project(turn):
        wait_bytes(mech_in.at[pl.ds(turn * group, group)], mech_rsem.at[turn])
        gathered = mech_in[pl.ds(turn * group, group)].reshape(group, 128)
        for column in range(12):
            wide[column] = jnp.broadcast_to(gathered[:, column : column + 1], (group, freqs))

        @pl.loop(0, group, unroll=2)
        def _(index):
            place = turn * group + index
            worker = lax.rem(place, nx) * nz + lax.rem(my_z + place // nx + nz - 1, nz)
            blocks = []
            for k in range(2):
                point = table_smem[worker // packs, lax.rem(worker, packs) * 2 + k]
                weights = [
                    jnp.broadcast_to(wide[k * 6 + m, pl.ds(index, 1), :], (sites, freqs)) for m in range(6)
                ]
                for part_id in range(2):
                    for c in range(2):
                        total = weights[0] * sgt[point, part_id, c, 0].astype(jnp.float32)
                        for m in range(1, 6):
                            total = total + weights[m] * sgt[point, part_id, c, m].astype(jnp.float32)
                        blocks.append(total)
            turned = jnp.concatenate(blocks, axis=0).T
            flip[pl.ds(index, freqs, stride=group), :] = turned

    def near_copy(step):
        x = lax.rem(my_x + step, nx)
        return pltpu.make_async_remote_copy(
            src_ref=near_out.at[x], dst_ref=near_in.at[my_x], send_sem=near_ssem, recv_sem=near_rsem,
            device_id={"sub": x * nz + my_z}, device_id_type=MESH,
        )

    def far_copy(i, step):
        x = lax.rem(my_x + step, nx)
        return pltpu.make_async_remote_copy(
            src_ref=far_out.at[i, x], dst_ref=far_in.at[i, my_x], send_sem=far_ssem.at[i],
            recv_sem=far_rsem.at[i], device_id={"sub": x * nz + my_z}, device_id_type=MESH,
        )

    def ring_copy(h, step):
        piece = pieces.at[h, site]
        return pltpu.make_async_remote_copy(
            src_ref=piece, dst_ref=piece, send_sem=ring_ssem.at[h, step - 1],
            recv_sem=ring_rsem.at[h, step - 1], device_id={"site": site_of(step)}, device_id_type=MESH,
        )

    def pair_copy(h, y):
        piece = pieces.at[h, y * 2 + core]
        return pltpu.make_async_remote_copy(
            src_ref=piece, dst_ref=piece, send_sem=pair_ssem.at[h], recv_sem=pair_rsem.at[h],
            device_id={"site": other}, device_id_type=MESH,
        )

    hops = sorted(range(1, nx), key=lambda dx: -min(dx, nx - dx))

    def send_near():
        for x in range(nx):
            rows = share * group
            near_out[x] = flip[pl.ds(x * rows, rows), :].astype(jnp.bfloat16).reshape(share, group, 2 * rows_pc)
        for step in hops:
            near_copy(step).start()
        pltpu.make_async_copy(near_out.at[my_x], near_in.at[my_x], near_rsem).start()

    def send_far():
        for i in range(cuts):
            for x in range(nx):
                rows = cut * group
                block = flip[pl.ds((x * cuts + i) * rows, rows), :].astype(jnp.bfloat16)
                far_out[i, x] = block.reshape(cut, group, 2 * rows_pc)
            for step in hops:
                far_copy(i, step).start()
            pltpu.make_async_copy(far_out.at[i, my_x], far_in.at[i, my_x], far_rsem.at[i]).start()

    def share_slip(h):
        wait_bytes(slip_in.at[h], slip_rsem.at[h])
        for place in range(workers):
            piece_flip[pl.ds(place, half, stride=workers), :] = slip_in[h, place].astype(jnp.float32)
        pieces[h, site] = piece_flip[...].astype(jnp.bfloat16).reshape(half, workers, vq)
        for step in range(1, ny):
            ring_copy(h, step).start()
        pair_copy(h, my_y).start()

    def pass_on(h):
        for step in range(1, ny):
            y = lax.rem(my_y + ny - step, ny)
            wait_bytes(pieces.at[h, y * 2 + core], ring_rsem.at[h, step - 1])
            pair_copy(h, y).start()

    lane = lax.broadcasted_iota(jnp.int32, (rows_pc // 2, vq), 1)
    even = lane % 2 == 0

    def contract(i):
        wait_bytes(far_in.at[i], far_rsem.at[i])
        for quad in range(quads):
            blocks = []
            for inner in range(4):
                f = quad * 4 + inner
                whole = i * cut + f
                projected = jnp.concatenate(
                    [near_in[x, whole] for x in range(nx)] + [far_in[i, x, f] for x in range(nx)], axis=0
                ).T
                left = jnp.concatenate([projected[:rows_pc], projected[rows_pc:]], axis=1)
                right = jnp.concatenate(
                    [
                        pieces[whole // half, k * nx + x, whole % half, pl.ds(turn * group, group), :]
                        for k in range(2)
                        for turn in range(2)
                        for x in range(nx)
                    ],
                    axis=0,
                )
                both = jnp.dot(left, right, preferred_element_type=jnp.float32)
                straight, crossed = both[: rows_pc // 2], both[rows_pc // 2 :]
                swapped = jnp.where(even, -pltpu.roll(crossed, vq - 1, 1), pltpu.roll(crossed, 1, 1))
                blocks.append(straight + swapped)
            part[i, pl.ds(quad, vq, stride=quads), :] = jnp.concatenate(blocks, axis=0).T
        part_out[i] = part[i].astype(jnp.bfloat16).reshape(workers, 4 * quads, 128)

        def send_part(x, z, place):
            pltpu.make_async_remote_copy(
                src_ref=part_out.at[i, x * nz + z], dst_ref=part_in.at[i, me], send_sem=part_ssem,
                recv_sem=part_rsem.at[i], device_id={"sub": x * nz + z}, device_id_type=MESH,
            ).start()

        each_peer(send_part)
        pltpu.make_async_copy(part_out.at[i, me], part_in.at[i, me], part_rsem.at[i]).start()

    project(0)
    send_near()
    share_slip(0)
    project(1)
    send_far()
    for h in range(1, halves):
        share_slip(h)
    pass_on(0)
    wait_bytes(near_in, near_rsem)
    for i in range(cuts):
        if i % (cuts // halves) == 0:
            h = i // (cuts // halves)
            if h:
                pass_on(h)
            wait_bytes(pieces.at[h, pl.ds(0, ny)], pair_rsem.at[h])
        contract(i)

    wait_bytes(mech_out.at[pl.ds(0, workers - 1)], mech_ssem)
    wait_bytes(slip_out.at[:, pl.ds(0, workers - 1)], slip_ssem)
    wait_bytes(near_out.at[pl.ds(0, nx - 1)], near_ssem)
    for i in range(cuts):
        wait_bytes(far_out.at[i, pl.ds(0, nx - 1)], far_ssem.at[i])
    for h in range(halves):
        for step in range(1, ny):
            wait_bytes(pieces.at[h, site], ring_ssem.at[h, step - 1])
        wait_bytes(pieces.at[h, pl.ds(0, ny)], pair_ssem.at[h])

    for i in range(cuts):
        wait_bytes(part_in.at[i], part_rsem.at[i])
        for x in range(nx):
            total = part_in[i, x * nz].astype(jnp.float32)
            for z in range(1, nz):
                total = total + part_in[i, x * nz + z].astype(jnp.float32)
            for row in range(4):
                sums[row, pl.ds((x * cuts + i) * quads, quads), :] = total[row * quads : (row + 1) * quads]
    rows = rows_pc // 2
    for e in range(2):
        for q in range(2):
            turned = sums[e * 2 + q].T
            spec_ref[e, q] = jnp.concatenate([turned[i * rows : (i + 1) * rows] for i in range(4)], axis=1)
    wait_bytes(part_out.at[:, pl.ds(0, workers - 1)], part_ssem)


def spectrum_call(dims, sgt, mechanism, slip, point_list, subfault_counts):
    nx, nz, ny = dims
    workers = nx * nz
    slots, variations, _, freqs = slip.shape
    vq = variations * 2
    rows_pc = 4 * sgt.shape[4]
    share = freqs // nx
    group = workers // 2
    half, cut = share // HALVES, share // CUTS
    quads = cut // 4
    packs = max(1, min(128 // slots, 2))
    table_rows = workers // packs
    points = point_list.reshape(table_rows, packs * slots)
    bf16, f32 = jnp.bfloat16, jnp.float32
    dma = pltpu.SemaphoreType.DMA
    hbm = pl.BlockSpec(memory_space=pltpu.HBM)
    operands = (points, subfault_counts, mechanism.T, slip.reshape(slots, vq, freqs), sgt)
    return pl.pallas_call(
        functools.partial(spectrum_kernel, dims),
        out_shape=jax.ShapeDtypeStruct((2, 2, rows_pc // 2, freqs), f32),
        in_specs=[hbm] * 5,
        out_specs=pl.BlockSpec(memory_space=pltpu.VMEM),
        scratch_shapes=[
            pltpu.VMEM(points.shape, jnp.int32),
            pltpu.SMEM(subfault_counts.shape, jnp.int32),
            pltpu.VMEM((6, slots), f32),
            pltpu.VMEM((table_rows + workers, 128), jnp.int32),
            pltpu.SMEM((table_rows + workers, 128), jnp.int32),
            pltpu.VMEM(sgt.shape, bf16),
            pltpu.VMEM((slots, vq, freqs), bf16),
            pltpu.VMEM((workers, 1, 128), f32),
            pltpu.VMEM((workers, 1, 128), f32),
            pltpu.VMEM((12, group, freqs), f32),
            pltpu.VMEM((HALVES, workers, half, vq), bf16),
            pltpu.VMEM((HALVES, workers, half, vq), bf16),
            pltpu.VMEM((freqs * group, 2 * rows_pc), f32),
            pltpu.VMEM((nx, share, group, 2 * rows_pc), bf16),
            pltpu.VMEM((nx, share, group, 2 * rows_pc), bf16),
            pltpu.VMEM((CUTS, nx, cut, group, 2 * rows_pc), bf16),
            pltpu.VMEM((CUTS, nx, cut, group, 2 * rows_pc), bf16),
            pltpu.VMEM((HALVES, ny * 2, half, workers, vq), bf16),
            pltpu.VMEM((half * workers, vq), f32),
            pltpu.VMEM((CUTS, vq * quads, 128), f32),
            pltpu.VMEM((CUTS, workers, 4 * quads, 128), bf16),
            pltpu.VMEM((CUTS, workers, 4 * quads, 128), bf16),
            pltpu.VMEM((4, share // 4 * nx, 128), f32),
            dma((3,)), dma, dma, dma, dma, dma((2,)), dma, dma((HALVES,)), dma, dma, dma((CUTS,)), dma((CUTS,)),
            dma((HALVES, ny - 1)), dma((HALVES, ny - 1)), dma((HALVES,)), dma((HALVES,)), dma, dma((CUTS,)),
        ],
        compiler_params=pltpu.CompilerParams(
            collective_id=0, has_side_effects=True, vmem_limit_bytes=36 * 1024 * 1024
        ),
        name="spectrum",
    )(*(pltpu.with_memory_space_constraint(x, pltpu.HBM) for x in operands))


def synthesis_kernel(
    spec_ref, gain_ref, high, low, seis_hbm, psa_ref, rows_in, peak, seis, put_sem
):
    tiles, _, tile = high.shape
    periods, freqs = gain_ref.shape[1:]
    rows = spec_ref.shape[2] * 2
    pair = 2 * rows
    per = periods // PARTS

    def put(t):
        return pltpu.make_async_copy(seis.at[t], seis_hbm.at[:, pl.ds(t * tile, tile)], put_sem.at[t])


    real = jnp.concatenate([spec_ref[0, 0], spec_ref[1, 0]], axis=0)
    imag = jnp.concatenate([spec_ref[0, 1], spec_ref[1, 1]], axis=0)
    spectrum = jnp.concatenate([real, imag], axis=1)
    top = spectrum.astype(jnp.bfloat16)
    rows_in[pl.ds(0, rows), :] = top
    rows_in[pl.ds(rows, rows), :] = (spectrum - top.astype(jnp.float32)).astype(jnp.bfloat16)

    def respond(start):
        for place in range(start, start + per):
            q = place // 2 + (place % 2) * (periods // 2)
            g0 = gain_ref[0, q : q + 1, :]
            g1 = gain_ref[1, q : q + 1, :]
            at = pl.ds(pair + place * rows, rows)
            rows_in[at, pl.ds(0, freqs)] = (g0 * real - g1 * imag).astype(jnp.bfloat16)
            rows_in[at, pl.ds(freqs, freqs)] = (g0 * imag + g1 * real).astype(jnp.bfloat16)

    def tile_step(t, opening=False, closing=False):
        found = []
        for start in range(0, periods, per):
            if opening:
                respond(start)
            first = 0 if start == 0 else pair + start * rows
            last = pair + (start + per) * rows
            wave = jnp.dot(rows_in[first:last, :], high[t], preferred_element_type=jnp.float32)
            if start == 0:
                motion = wave[:rows] + wave[rows:pair]
                motion = motion + jnp.dot(rows_in[:rows, :], low[t], preferred_element_type=jnp.float32)
                seis[t] = motion.astype(jnp.bfloat16)
                wave = wave[pair:]
            wave = jnp.abs(wave)
            most = wave[:, :128]
            for column in range(128, tile, 128):
                most = jnp.maximum(most, wave[:, column : column + 128])
            part = pl.ds(start * rows, per * rows)
            if not opening:
                most = jnp.maximum(peak[part, :], most)
            if not closing:
                peak[part, :] = most
            else:
                for block in range(0, per * rows, pair):
                    found.append(jnp.max(most[block : block + pair].T, axis=0, keepdims=True))
        put(t).start()
        return found

    tile_step(0, opening=True)

    @pl.loop(1, tiles - 1)
    def _(t):
        tile_step(t)

    found = tile_step(tiles - 1, closing=True)
    both = jnp.concatenate(found, axis=0)
    psa_ref[...] = jnp.concatenate([both[:, :rows].T, both[:, rows:].T], axis=1)
    for t in range(tiles):
        put(t).wait()


def synthesis_call(spec):
    rows, freqs = 2 * spec.shape[2], spec.shape[3]
    high, low = (
        np.ascontiguousarray(a.reshape(2 * freqs, NT // TILE, TILE).swapaxes(0, 1)) for a in synthesis_basis(freqs, NT)
    )
    gains = oscillator_gains(PERIODS, freqs, NT)
    tiles = NT // TILE
    vmem, anywhere = pl.BlockSpec(memory_space=pltpu.VMEM), pl.BlockSpec(memory_space=pl.ANY)
    return pl.pallas_call(
        synthesis_kernel,
        out_shape=(
            jax.ShapeDtypeStruct((rows, NT), jnp.bfloat16),
            jax.ShapeDtypeStruct((rows, PERIODS), jnp.float32),
        ),
        in_specs=[vmem, vmem, vmem, vmem],
        out_specs=(anywhere, vmem),
        scratch_shapes=[
            pltpu.VMEM(((PERIODS + 2) * rows, 2 * freqs), jnp.bfloat16),
            pltpu.VMEM((PERIODS * rows, 128), jnp.float32),
            pltpu.VMEM((tiles, rows, TILE), jnp.bfloat16),
            pltpu.SemaphoreType.DMA((tiles,)),
        ],
        compiler_params=pltpu.CompilerParams(vmem_limit_bytes=36 * 1024 * 1024),
        name="synthesis",
    )(spec, jnp.asarray(gains), jnp.asarray(high), jnp.asarray(low))


def per_device(dims, sgt, mechanism, slip, point_list, subfault_counts):
    spec = spectrum_call(dims, sgt, mechanism, slip, point_list, subfault_counts)
    seis, psa = synthesis_call(spec)
    sites = sgt.shape[4]
    return seis.reshape(2, 2, sites, NT), psa.reshape(2, 2, sites, PERIODS)


def solution(mesh):
    workers, site_devices = mesh.shape["sub"], mesh.shape["site"]
    nx = site_devices // 2
    dims = (nx, workers // nx, site_devices // 2)
    in_specs = (
        P("sub", None, None, None, "site", None),
        P("sub", None),
        P("sub", None, None, None),
        P(),
        P(),
    )
    out_specs = (P("sub", None, "site", None), P("sub", None, "site", None))
    return jax.shard_map(
        functools.partial(per_device, dims), mesh=mesh, in_specs=in_specs, out_specs=out_specs, check_vma=False
    )
```

```python
import functools
import math

import jax
import jax.numpy as jnp
import numpy as np
from jax import lax
from jax.experimental import pallas as pl
from jax.experimental.pallas import tpu as pltpu
from jax.sharding import PartitionSpec as P

NT = 2048
PERIODS = 40
HALVES = 4
DEPTH = 2
CUTS = 4
PARTS = 5
TILE = 512
MESH = pl.DeviceIdType.MESH

damping = 0.05
sample_step = 0.1


def bins_in_order(freq_count):
    kappa = np.arange(freq_count)
    quarter = freq_count // 4
    return 4 * (kappa % quarter) + kappa // quarter


def synthesis_basis(freq_count, sample_count):
    freq_ids = bins_in_order(freq_count)
    angles = (freq_ids[:, None] * np.arange(sample_count)[None, :] % sample_count) * (2.0 * math.pi / sample_count)
    scale = 1.0 / math.sqrt(freq_count)
    both = np.concatenate([scale * np.cos(angles), -scale * np.sin(angles)], axis=0).astype(np.float32)
    high = both.astype(jnp.bfloat16)
    low = (both - high.astype(np.float32)).astype(jnp.bfloat16)
    return high, low


def oscillator_gains(period_count, freq_count, sample_count):
    periods = 2.0 * np.exp(np.arange(period_count) * (math.log(5.0) / max(period_count - 1, 1)))
    natural = 2.0 * math.pi / periods
    omega = bins_in_order(freq_count) * (2.0 * math.pi / (sample_count * sample_step))
    squared = (natural * natural)[:, None]
    real_part = squared - (omega * omega)[None, :]
    imag_part = 2.0 * damping * natural[:, None] * omega[None, :]
    magnitude = real_part * real_part + imag_part * imag_part
    return np.stack([-squared * real_part / magnitude, squared * imag_part / magnitude]).astype(np.float32)


def spectrum_kernel(
    dims, points_hbm, counts_hbm, mech_hbm, slip_hbm, sgt_hbm, spec_ref,
    points_ref, counts_ref, mech_ref, table, table_smem, sgt, slip, mech_out, mech_in, wide, slip_out, slip_in, flip, near_out, near_in, far_out, far_in,
    pieces, piece_flip, part, part_out, part_in, sums,
    small_sem, table_sem, sgt_sem, slip_sem, mech_ssem, mech_rsem, slip_ssem, slip_rsem, near_ssem, near_rsem, far_ssem, far_rsem,
    ring_ssem, ring_rsem, pair_ssem, pair_rsem, part_ssem, part_rsem,
):
    nx, nz, ny = dims
    workers = nx * nz
    slots, vq, freqs = slip.shape
    sites = sgt.shape[4]
    rows_pc = 4 * sites
    per_reader = sgt.shape[0]
    share = freqs // nx
    group = workers // 2
    packs = points_ref.shape[1] // slots
    table_rows = points_ref.shape[0]
    lanes = points_ref.shape[1]
    halves = slip_out.shape[0]
    half = share // halves
    cuts = far_out.shape[0]
    cut = share // cuts
    quads = cut // 4

    me = lax.axis_index("sub")
    site = lax.axis_index("site")
    my_x = me // nz
    my_z = lax.rem(me, nz)
    my_y = site // 2
    core = lax.rem(site, 2)
    other = my_y * 2 + (1 - core)

    small = [
        pltpu.make_async_copy(source, target, small_sem.at[i])
        for i, (source, target) in enumerate(
            ((points_hbm, points_ref), (counts_hbm, counts_ref), (mech_hbm, mech_ref))
        )
    ]
    for copy in small:
        copy.start()
    get_slip = pltpu.make_async_copy(slip_hbm, slip, slip_sem)
    get_slip.start()
    get_sgt = pltpu.make_async_copy(sgt_hbm, sgt, sgt_sem)
    get_sgt.start()

    def each_peer(act):
        xs = [lax.rem(my_x + dx, nx) for dx in range(nx)]
        order = sorted(range(nx), key=lambda dx: -min(dx, nx - dx))

        @pl.loop(0, nz - 1)
        def _(step):
            away = (step + 1) // 2
            dz = nz // 2 + jnp.where(lax.rem(step, 2) == 0, away, -away)
            z = lax.rem(my_z + dz, nz)
            place = lax.rem(nz - dz + 1, nz) * nx + my_x
            for dx in order:
                act(xs[dx], z, place)

        for dx in order:
            if dx:
                act(xs[dx], my_z, nx + my_x)

    my_place = nx + my_x

    def site_of(step):
        return lax.rem(my_y + step, ny) * 2 + core

    barrier = pltpu.get_barrier_semaphore()

    def greet(x, z, place):
        pl.semaphore_signal(barrier, inc=1, device_id={"sub": x * nz + z}, device_id_type=MESH)

    each_peer(greet)
    for step in range(1, ny):
        pl.semaphore_signal(barrier, inc=1, device_id={"site": site_of(step)}, device_id_type=MESH)
    pl.semaphore_signal(barrier, inc=1, device_id={"site": other}, device_id_type=MESH)

    for copy in small:
        copy.wait()
    points = points_ref[...]
    lane = lax.broadcasted_iota(jnp.int32, (table_rows, lanes), 1)
    out_lane = lax.broadcasted_iota(jnp.int32, (table_rows, 128), 1)
    mine = points // per_reader == me
    local = points % per_reader
    named = jnp.zeros((table_rows, 128), jnp.int32)
    for pack in range(packs):
        here = mine & (lane // slots == pack)
        first = jnp.min(jnp.where(here, lane, lanes), axis=1, keepdims=True)
        last = jnp.max(jnp.where(here, lane, -1), axis=1, keepdims=True)
        for k, found in enumerate((first, last)):
            row = jnp.sum(jnp.where(here & (lane == found), local, 0), axis=1, keepdims=True)
            named = jnp.where(out_lane == pack * 2 + k, row, named)
    table[pl.ds(0, table_rows), :] = named

    my_points = points_ref[pl.ds(me // packs, 1), :]
    lane = lax.broadcasted_iota(jnp.int32, (workers, lanes), 1)
    out_lane = lax.broadcasted_iota(jnp.int32, (workers, 128), 1)
    reader = lax.broadcasted_iota(jnp.int32, (workers, lanes), 0)
    base = lax.rem(me, packs) * slots
    here = (my_points // per_reader == reader) & (lane >= base) & (lane < base + slots)
    first = jnp.min(jnp.where(here, lane, lanes), axis=1, keepdims=True)
    last = jnp.max(jnp.where(here, lane, -1), axis=1, keepdims=True)
    table[pl.ds(table_rows, workers), :] = jnp.clip(jnp.where(out_lane == 0, first, last) - base, 0, slots - 1)
    to_smem = pltpu.make_async_copy(table, table_smem, table_sem)
    to_smem.start()

    live = lane - base < counts_ref[me]
    moments = jnp.concatenate([mech_ref[...]] * packs, axis=1)
    sent = jnp.zeros((workers, 128), jnp.float32)
    for k, found in enumerate((first, last)):
        chosen = here & live & (lane == found)
        for m in range(6):
            value = jnp.sum(jnp.where(chosen, moments[m : m + 1, :], 0.0), axis=1, keepdims=True)
            sent = jnp.where(out_lane == k * 6 + m, value, sent)
    mech_out[...] = sent.reshape(workers, 1, 128)

    to_smem.wait()
    get_slip.wait()
    my_k = site // nx
    x_of_piece = lax.rem(site, nx)

    @pl.loop(0, nz)
    def _(zr):
        slot = table_smem[table_rows + x_of_piece * nz + zr, my_k]
        turned = slip[slot].astype(jnp.float32).T.astype(jnp.bfloat16)
        for h in range(halves):
            for x in range(nx):
                start = x * share + h * half
                slip_out[h, x * nz + zr] = turned[start : start + half]

    get_sgt.wait()
    pl.semaphore_wait(barrier, workers - 1 + ny)

    def wait_bytes(ref, sem):
        pltpu.make_async_copy(ref, ref, sem).wait()

    def send_mech(x, z, place):
        pltpu.make_async_remote_copy(
            src_ref=mech_out.at[x * nz + z], dst_ref=mech_in.at[place], send_sem=mech_ssem,
            recv_sem=mech_rsem.at[place // group], device_id={"sub": x * nz + z}, device_id_type=MESH,
        ).start()

    each_peer(send_mech)
    pltpu.make_async_copy(mech_out.at[me], mech_in.at[my_place], mech_rsem.at[my_place // group]).start()

    for h in range(halves):

        def send_slip(x, z, place, h=h):
            pltpu.make_async_remote_copy(
                src_ref=slip_out.at[h, x * nz + z], dst_ref=slip_in.at[h, place], send_sem=slip_ssem,
                recv_sem=slip_rsem.at[h], device_id={"sub": x * nz + z}, device_id_type=MESH,
            ).start()

        each_peer(send_slip)
        pltpu.make_async_copy(slip_out.at[h, me], slip_in.at[h, my_place], slip_rsem.at[h]).start()

    def project(turn):
        wait_bytes(mech_in.at[pl.ds(turn * group, group)], mech_rsem.at[turn])
        gathered = mech_in[pl.ds(turn * group, group)].reshape(group, 128)
        for column in range(12):
            wide[column] = jnp.broadcast_to(gathered[:, column : column + 1], (group, freqs))

        @pl.loop(0, group, unroll=4)
        def _(index):
            place = turn * group + index
            worker = lax.rem(place, nx) * nz + lax.rem(my_z + place // nx + nz - 1, nz)
            blocks = []
            for k in range(2):
                point = table_smem[worker // packs, lax.rem(worker, packs) * 2 + k]
                weights = [
                    jnp.broadcast_to(wide[k * 6 + m, pl.ds(index, 1), :], (sites, freqs)) for m in range(6)
                ]
                for part_id in range(2):
                    for c in range(2):
                        total = weights[0] * sgt[point, part_id, c, 0].astype(jnp.float32)
                        for m in range(1, 6):
                            total = total + weights[m] * sgt[point, part_id, c, m].astype(jnp.float32)
                        blocks.append(total)
            turned = jnp.concatenate(blocks, axis=0).T
            flip[pl.ds(index, freqs, stride=group), :] = turned

    def near_copy(step):
        x = lax.rem(my_x + step, nx)
        return pltpu.make_async_remote_copy(
            src_ref=near_out.at[x], dst_ref=near_in.at[my_x], send_sem=near_ssem, recv_sem=near_rsem,
            device_id={"sub": x * nz + my_z}, device_id_type=MESH,
        )

    def far_copy(i, step):
        x = lax.rem(my_x + step, nx)
        return pltpu.make_async_remote_copy(
            src_ref=far_out.at[i, x], dst_ref=far_in.at[i, my_x], send_sem=far_ssem.at[i],
            recv_sem=far_rsem.at[i], device_id={"sub": x * nz + my_z}, device_id_type=MESH,
        )

    def ring_copy(h, step):
        piece = pieces.at[h, site]
        return pltpu.make_async_remote_copy(
            src_ref=piece, dst_ref=piece, send_sem=ring_ssem.at[h, step - 1],
            recv_sem=ring_rsem.at[h, step - 1], device_id={"site": site_of(step)}, device_id_type=MESH,
        )

    def pair_copy(h, y):
        piece = pieces.at[h, y * 2 + core]
        return pltpu.make_async_remote_copy(
            src_ref=piece, dst_ref=piece, send_sem=pair_ssem.at[h], recv_sem=pair_rsem.at[h],
            device_id={"site": other}, device_id_type=MESH,
        )

    hops = sorted(range(1, nx), key=lambda dx: -min(dx, nx - dx))

    def send_near():
        for x in range(nx):
            rows = share * group
            near_out[x] = flip[pl.ds(x * rows, rows), :].astype(jnp.bfloat16).reshape(share, group, 2 * rows_pc)
        for step in hops:
            near_copy(step).start()
        pltpu.make_async_copy(near_out.at[my_x], near_in.at[my_x], near_rsem).start()

    def send_far():
        for i in range(cuts):
            for x in range(nx):
                rows = cut * group
                block = flip[pl.ds((x * cuts + i) * rows, rows), :].astype(jnp.bfloat16)
                far_out[i, x] = block.reshape(cut, group, 2 * rows_pc)
            for step in hops:
                far_copy(i, step).start()
            pltpu.make_async_copy(far_out.at[i, my_x], far_in.at[i, my_x], far_rsem.at[i]).start()

    def share_slip(h):
        wait_bytes(slip_in.at[h], slip_rsem.at[h])
        for place in range(workers):
            piece_flip[pl.ds(place, half, stride=workers), :] = slip_in[h, place].astype(jnp.float32)
        pieces[h, site] = piece_flip[...].astype(jnp.bfloat16).reshape(half, workers, vq)
        pair_copy(h, my_y).start()

    ring_steps = sorted(range(1, ny), key=lambda dy: -min(dy, ny - dy))

    def sent_ring(h):
        for step in ring_steps:
            wait_bytes(pieces.at[h, site], ring_ssem.at[h, step - 1])

    def launch(h):
        if h >= DEPTH:
            sent_ring(h - DEPTH)
        for step in ring_steps:
            ring_copy(h, step).start()

    def pass_on(h):
        for step in reversed(ring_steps):
            y = lax.rem(my_y + ny - step, ny)
            wait_bytes(pieces.at[h, y * 2 + core], ring_rsem.at[h, step - 1])
            pair_copy(h, y).start()

    lane = lax.broadcasted_iota(jnp.int32, (rows_pc // 2, vq), 1)
    even = lane % 2 == 0

    def contract(i):
        wait_bytes(far_in.at[i], far_rsem.at[i])
        for quad in range(quads):
            blocks = []
            for inner in range(4):
                f = quad * 4 + inner
                whole = i * cut + f
                projected = jnp.concatenate(
                    [near_in[x, whole] for x in range(nx)] + [far_in[i, x, f] for x in range(nx)], axis=0
                ).T
                left = jnp.concatenate([projected[:rows_pc], projected[rows_pc:]], axis=1)
                right = jnp.concatenate(
                    [
                        pieces[whole // half, k * nx + x, whole % half, pl.ds(turn * group, group), :]
                        for k in range(2)
                        for turn in range(2)
                        for x in range(nx)
                    ],
                    axis=0,
                )
                both = jnp.dot(left, right, preferred_element_type=jnp.float32)
                straight, crossed = both[: rows_pc // 2], both[rows_pc // 2 :]
                swapped = jnp.where(even, -pltpu.roll(crossed, vq - 1, 1), pltpu.roll(crossed, 1, 1))
                blocks.append(straight + swapped)
            part[i, pl.ds(quad, vq, stride=quads), :] = jnp.concatenate(blocks, axis=0).T
        part_out[i] = part[i].astype(jnp.bfloat16).reshape(workers, 4 * quads, 128)

        def send_part(x, z, place):
            pltpu.make_async_remote_copy(
                src_ref=part_out.at[i, x * nz + z], dst_ref=part_in.at[i, me], send_sem=part_ssem,
                recv_sem=part_rsem.at[i], device_id={"sub": x * nz + z}, device_id_type=MESH,
            ).start()

        each_peer(send_part)
        pltpu.make_async_copy(part_out.at[i, me], part_in.at[i, me], part_rsem.at[i]).start()

    project(0)
    send_near()
    share_slip(0)
    launch(0)
    project(1)
    send_far()
    for h in range(1, halves):
        share_slip(h)
        if h < DEPTH:
            launch(h)
    for h in range(DEPTH, halves):
        launch(h)
        pass_on(h - DEPTH)
    wait_bytes(near_in, near_rsem)
    for i in range(cuts):
        if i % (cuts // halves) == 0:
            h = i // (cuts // halves)
            if h >= halves - DEPTH:
                pass_on(h)
            wait_bytes(pieces.at[h, pl.ds(0, ny)], pair_rsem.at[h])
        contract(i)

    wait_bytes(mech_out.at[pl.ds(0, workers - 1)], mech_ssem)
    wait_bytes(slip_out.at[:, pl.ds(0, workers - 1)], slip_ssem)
    wait_bytes(near_out.at[pl.ds(0, nx - 1)], near_ssem)
    for i in range(cuts):
        wait_bytes(far_out.at[i, pl.ds(0, nx - 1)], far_ssem.at[i])
    for h in range(halves):
        if h >= halves - DEPTH:
            sent_ring(h)
        wait_bytes(pieces.at[h, pl.ds(0, ny)], pair_ssem.at[h])

    for i in range(cuts):
        wait_bytes(part_in.at[i], part_rsem.at[i])
        for x in range(nx):
            total = part_in[i, x * nz].astype(jnp.float32)
            for z in range(1, nz):
                total = total + part_in[i, x * nz + z].astype(jnp.float32)
            for row in range(4):
                sums[row, pl.ds((x * cuts + i) * quads, quads), :] = total[row * quads : (row + 1) * quads]
    rows = rows_pc // 2
    for e in range(2):
        for q in range(2):
            turned = sums[e * 2 + q].T
            spec_ref[e, q] = jnp.concatenate([turned[i * rows : (i + 1) * rows] for i in range(4)], axis=1)
    wait_bytes(part_out.at[:, pl.ds(0, workers - 1)], part_ssem)


def spectrum_call(dims, sgt, mechanism, slip, point_list, subfault_counts):
    nx, nz, ny = dims
    workers = nx * nz
    slots, variations, _, freqs = slip.shape
    vq = variations * 2
    rows_pc = 4 * sgt.shape[4]
    share = freqs // nx
    group = workers // 2
    half, cut = share // HALVES, share // CUTS
    quads = cut // 4
    packs = max(1, min(128 // slots, 2))
    table_rows = workers // packs
    points = point_list.reshape(table_rows, packs * slots)
    bf16, f32 = jnp.bfloat16, jnp.float32
    dma = pltpu.SemaphoreType.DMA
    hbm = pl.BlockSpec(memory_space=pltpu.HBM)
    operands = (points, subfault_counts, mechanism.T, slip.reshape(slots, vq, freqs), sgt)
    return pl.pallas_call(
        functools.partial(spectrum_kernel, dims),
        out_shape=jax.ShapeDtypeStruct((2, 2, rows_pc // 2, freqs), f32),
        in_specs=[hbm] * 5,
        out_specs=pl.BlockSpec(memory_space=pltpu.VMEM),
        scratch_shapes=[
            pltpu.VMEM(points.shape, jnp.int32),
            pltpu.SMEM(subfault_counts.shape, jnp.int32),
            pltpu.VMEM((6, slots), f32),
            pltpu.VMEM((table_rows + workers, 128), jnp.int32),
            pltpu.SMEM((table_rows + workers, 128), jnp.int32),
            pltpu.VMEM(sgt.shape, bf16),
            pltpu.VMEM((slots, vq, freqs), bf16),
            pltpu.VMEM((workers, 1, 128), f32),
            pltpu.VMEM((workers, 1, 128), f32),
            pltpu.VMEM((12, group, freqs), f32),
            pltpu.VMEM((HALVES, workers, half, vq), bf16),
            pltpu.VMEM((HALVES, workers, half, vq), bf16),
            pltpu.VMEM((freqs * group, 2 * rows_pc), f32),
            pltpu.VMEM((nx, share, group, 2 * rows_pc), bf16),
            pltpu.VMEM((nx, share, group, 2 * rows_pc), bf16),
            pltpu.VMEM((CUTS, nx, cut, group, 2 * rows_pc), bf16),
            pltpu.VMEM((CUTS, nx, cut, group, 2 * rows_pc), bf16),
            pltpu.VMEM((HALVES, ny * 2, half, workers, vq), bf16),
            pltpu.VMEM((half * workers, vq), f32),
            pltpu.VMEM((CUTS, vq * quads, 128), f32),
            pltpu.VMEM((CUTS, workers, 4 * quads, 128), bf16),
            pltpu.VMEM((CUTS, workers, 4 * quads, 128), bf16),
            pltpu.VMEM((4, share // 4 * nx, 128), f32),
            dma((3,)), dma, dma, dma, dma, dma((2,)), dma, dma((HALVES,)), dma, dma, dma((CUTS,)), dma((CUTS,)),
            dma((HALVES, ny - 1)), dma((HALVES, ny - 1)), dma((HALVES,)), dma((HALVES,)), dma, dma((CUTS,)),
        ],
        compiler_params=pltpu.CompilerParams(
            collective_id=0, has_side_effects=True, vmem_limit_bytes=36 * 1024 * 1024
        ),
        name="spectrum",
    )(*(pltpu.with_memory_space_constraint(x, pltpu.HBM) for x in operands))


def synthesis_kernel(
    spec_ref, gain_ref, high, low, seis_hbm, psa_ref, rows_in, peak, seis, put_sem
):
    tiles, _, tile = high.shape
    periods, freqs = gain_ref.shape[1:]
    rows = spec_ref.shape[2] * 2
    pair = 2 * rows
    per = periods // PARTS

    def put(t):
        return pltpu.make_async_copy(seis.at[t], seis_hbm.at[:, pl.ds(t * tile, tile)], put_sem.at[t])


    real = jnp.concatenate([spec_ref[0, 0], spec_ref[1, 0]], axis=0)
    imag = jnp.concatenate([spec_ref[0, 1], spec_ref[1, 1]], axis=0)
    spectrum = jnp.concatenate([real, imag], axis=1)
    top = spectrum.astype(jnp.bfloat16)
    rows_in[pl.ds(0, rows), :] = top
    rows_in[pl.ds(rows, rows), :] = (spectrum - top.astype(jnp.float32)).astype(jnp.bfloat16)

    def respond(start):
        for place in range(start, start + per):
            q = place // 2 + (place % 2) * (periods // 2)
            g0 = gain_ref[0, q : q + 1, :]
            g1 = gain_ref[1, q : q + 1, :]
            at = pl.ds(pair + place * rows, rows)
            rows_in[at, pl.ds(0, freqs)] = (g0 * real - g1 * imag).astype(jnp.bfloat16)
            rows_in[at, pl.ds(freqs, freqs)] = (g0 * imag + g1 * real).astype(jnp.bfloat16)

    def tile_step(t, opening=False, closing=False):
        found = []
        for start in range(0, periods, per):
            if opening:
                respond(start)
            first = 0 if start == 0 else pair + start * rows
            last = pair + (start + per) * rows
            wave = jnp.dot(rows_in[first:last, :], high[t], preferred_element_type=jnp.float32)
            if start == 0:
                motion = wave[:rows] + wave[rows:pair]
                motion = motion + jnp.dot(rows_in[:rows, :], low[t], preferred_element_type=jnp.float32)
                seis[t] = motion.astype(jnp.bfloat16)
                wave = wave[pair:]
            wave = jnp.abs(wave)
            most = wave[:, :128]
            for column in range(128, tile, 128):
                most = jnp.maximum(most, wave[:, column : column + 128])
            part = pl.ds(start * rows, per * rows)
            if not opening:
                most = jnp.maximum(peak[part, :], most)
            if not closing:
                peak[part, :] = most
            else:
                for block in range(0, per * rows, pair):
                    found.append(jnp.max(most[block : block + pair].T, axis=0, keepdims=True))
        put(t).start()
        return found

    tile_step(0, opening=True)

    @pl.loop(1, tiles - 1)
    def _(t):
        tile_step(t)

    found = tile_step(tiles - 1, closing=True)
    both = jnp.concatenate(found, axis=0)
    psa_ref[...] = jnp.concatenate([both[:, :rows].T, both[:, rows:].T], axis=1)
    for t in range(tiles):
        put(t).wait()


def synthesis_call(spec):
    rows, freqs = 2 * spec.shape[2], spec.shape[3]
    high, low = (
        np.ascontiguousarray(a.reshape(2 * freqs, NT // TILE, TILE).swapaxes(0, 1)) for a in synthesis_basis(freqs, NT)
    )
    gains = oscillator_gains(PERIODS, freqs, NT)
    tiles = NT // TILE
    vmem, anywhere = pl.BlockSpec(memory_space=pltpu.VMEM), pl.BlockSpec(memory_space=pl.ANY)
    return pl.pallas_call(
        synthesis_kernel,
        out_shape=(
            jax.ShapeDtypeStruct((rows, NT), jnp.bfloat16),
            jax.ShapeDtypeStruct((rows, PERIODS), jnp.float32),
        ),
        in_specs=[vmem, vmem, vmem, vmem],
        out_specs=(anywhere, vmem),
        scratch_shapes=[
            pltpu.VMEM(((PERIODS + 2) * rows, 2 * freqs), jnp.bfloat16),
            pltpu.VMEM((PERIODS * rows, 128), jnp.float32),
            pltpu.VMEM((tiles, rows, TILE), jnp.bfloat16),
            pltpu.SemaphoreType.DMA((tiles,)),
        ],
        compiler_params=pltpu.CompilerParams(vmem_limit_bytes=36 * 1024 * 1024),
        name="synthesis",
    )(spec, jnp.asarray(gains), jnp.asarray(high), jnp.asarray(low))


def per_device(dims, sgt, mechanism, slip, point_list, subfault_counts):
    spec = spectrum_call(dims, sgt, mechanism, slip, point_list, subfault_counts)
    seis, psa = synthesis_call(spec)
    sites = sgt.shape[4]
    return seis.reshape(2, 2, sites, NT), psa.reshape(2, 2, sites, PERIODS)


def solution(mesh):
    workers, site_devices = mesh.shape["sub"], mesh.shape["site"]
    nx = site_devices // 2
    dims = (nx, workers // nx, site_devices // 2)
    in_specs = (
        P("sub", None, None, None, "site", None),
        P("sub", None),
        P("sub", None, None, None),
        P(),
        P(),
    )
    out_specs = (P("sub", None, "site", None), P("sub", None, "site", None))
    return jax.shard_map(
        functools.partial(per_device, dims), mesh=mesh, in_specs=in_specs, out_specs=out_specs, check_vma=False
    )
```
